32 devices in a mesh: gx: 4 (over y, core), gy: 8 (over z, x).
Axes of the slice: x: 2, y: 2, z: 4, core: 2. Of those that a mesh axis runs over, the one named last changes fastest.
Arguments:
- image: bfloat16 [6960, 1536], P('gy', 'gx'), may hold values from -40 to 40
- text: bfloat16 [1232, 1536], P('gy', 'gx'), may hold values from -40 to 40
- condition: bfloat16 [8, 1536], P(None, 'gy'), may hold values from -6 to 6
- attend_weight: bfloat16 [1, 2, 1536, 3, 1536], P(None, None, 'gy', None, 'gx'), may hold values from -2 to 2
- output_weight: bfloat16 [1, 2, 1536, 1536], P(None, None, 'gx', 'gy'), may hold values from -2.5 to 2.5
- up_weight: bfloat16 [1, 2, 1536, 6144], P(None, None, 'gy', 'gx'), may hold values from -0.15625 to 0.15625
- down_weight: bfloat16 [1, 2, 6144, 1536], P(None, None, 'gx', 'gy'), may hold values from -0.15625 to 0.15625
- adaptive_weight: bfloat16 [1, 2, 1536, 6, 1536], P(None, None, 'gy', None, 'gx'), may hold values from -0.15625 to 0.15625
- image_cotangent: bfloat16 [6960, 1536], P('gy', 'gx'), may hold values from -6 to 6
- text_cotangent: bfloat16 [1232, 1536], P('gy', 'gx'), may hold values from -6 to 6
Outputs:
- image_result: bfloat16 [6960, 1536], P('gy', 'gx')
- text_result: bfloat16 [1232, 1536], P('gy', 'gx')
- image_grad: float32 [6960, 1536], P('gy', 'gx')
- text_grad: float32 [1232, 1536], P('gy', 'gx')
- condition_grad: float32 [8, 1536], P('gx', 'gy')
- attend_grad: float32 [1, 2, 1536, 3, 1536], P(None, None, 'gy', None, 'gx')
- output_grad: float32 [1, 2, 1536, 1536], P(None, None, 'gx', 'gy')
- up_grad: float32 [1, 2, 1536, 6144], P(None, None, 'gy', 'gx')
- down_grad: float32 [1, 2, 6144, 1536], P(None, None, 'gx', 'gy')
- adaptive_grad: float32 [1, 2, 1536, 6, 1536], P(None, None, 'gy', None, 'gx')
The draws below stay inside these ranges and needn't reach their ends.
All inputs are finite; a program needn't handle non-finite values.
Results may differ from the reference program's by a relative error of at most 0.02.
The reference program's roundings to bfloat16 on the way count: a program that leaves them out, or rounds other values in their place, can miss the bound.
Values may be sent and summed in bfloat16 or wider, within the bound.
No kernel may reach another device: no remote copies, remote signals or barrier semaphores. Data moves between devices by JAX's collectives and lax.ppermute only.
A program may use at most 192 MiB of HBM per device.

```python
import jax
import jax.numpy as jnp
from jax import lax

D = 1536
HEADS = 24
HD = 64
FF = 6144
IMG = 870
TXT = 154
BLOCKS = 1
LEN = 1024
SEQS = 8


def column_scales():
    columns = jnp.arange(D, dtype=jnp.float32) / (D - 1)
    return 10.0 ** (columns - 0.5)


def draw_activation(key, row_count):
    first_key, second_key = jax.random.split(key, 2)
    row_scale = 10.0 ** (jax.random.uniform(second_key, (row_count, 1), dtype=jnp.float32) - 0.5)
    values = jnp.clip(jax.random.normal(first_key, (row_count, D), dtype=jnp.float32), -4.0, 4.0)
    return values * column_scales() * row_scale


def draw_image(key, part):
    return draw_activation(key, SEQS * IMG).astype(jnp.bfloat16)


def draw_text(key, part):
    return draw_activation(key, SEQS * TXT).astype(jnp.bfloat16)


def draw_attend_weight(key, part):
    first_key, second_key, third_key = jax.random.split(key, 3)
    full_shape = (BLOCKS, 2, D, 1, D)
    spread_scale = D ** (-0.5)
    value_part = jnp.clip(jax.random.normal(third_key, full_shape, dtype=jnp.float32), -4.0, 4.0) * spread_scale
    queries = jnp.clip(jax.random.normal(first_key, full_shape, dtype=jnp.float32), -4.0, 4.0) * spread_scale
    key_part = jnp.clip(jax.random.normal(second_key, full_shape, dtype=jnp.float32), -4.0, 4.0) * spread_scale
    return jnp.concatenate([queries, key_part, value_part], axis=3).astype(jnp.bfloat16)


def steps_of(stream_key, extent, cuts, least, high):
    gain, own = 1.0, jax.random.fold_in(stream_key, 6)
    for position, blocks in cuts:
        heights = jnp.exp(jax.random.uniform(jax.random.fold_in(own, position), (blocks,), jnp.float32, least / len(cuts), high / len(cuts)))
        gain = gain * jnp.repeat(heights, extent[position] // blocks).reshape([-1 if axis == position else 1 for axis in range(len(extent))])
    return gain


def gaussian(own_key, dims, width, reach, shards=(), kind=jnp.bfloat16):
    array = width * jax.random.normal(own_key, dims, jnp.float32)
    if shards:
        array = array * steps_of(own_key, dims, shards, -0.22, 0.18)
    return jnp.clip(array, -reach, reach).astype(kind)


def setup_inputs(seed: int = 0) -> dict:
    splits = jax.random.split(jax.random.key(seed), 11)
    return {
        "image": draw_image(jax.random.fold_in(splits[10], 71), 0),
        "text": draw_text(jax.random.fold_in(splits[10], 71), 0),
        "condition": gaussian(splits[2], (SEQS, D), 1.0, 6.0, ((1, 8),)),
        "attend_weight": draw_attend_weight(jax.random.fold_in(splits[10], 71), 0),
        "output_weight": gaussian(splits[4], (BLOCKS, 2, D, D), (max(D // 256, 1)) ** -0.5, 2.5, ((2, 4), (3, 8))),
        "up_weight": gaussian(splits[5], (BLOCKS, 2, D, FF), D ** -0.5, 0.15625, ((2, 8), (3, 4))),
        "down_weight": gaussian(splits[6], (BLOCKS, 2, FF, D), (FF // 4) ** -0.5, 0.15625, ((2, 4), (3, 8))),
        "adaptive_weight": gaussian(splits[7], (BLOCKS, 2, D, 6, D), D ** -0.5, 0.15625, ((2, 8), (4, 4))),
        "image_cotangent": gaussian(splits[8], (SEQS * IMG, D), 1.0, 6.0, ((0, 8), (1, 4))),
        "text_cotangent": gaussian(splits[9], (SEQS * TXT, D), 1.0, 6.0, ((0, 8), (1, 4))),
    }


@jax.custom_vjp
def low(v):
    return lax.optimization_barrier(v.astype(jnp.bfloat16)).astype(jnp.float32)

@jax.custom_vjp
def low_back(v):
    return v

def low_keep(v):
    return (low(v), None)

def low_pass(kept, grad):
    return (grad,)

def back_keep(v):
    return (v, None)

def back_low(kept, grad):
    return (low(grad),)
low.defvjp(low_keep, low_pass)
low_back.defvjp(back_keep, back_low)

def layer_norm(values):
    average = lax.optimization_barrier(jnp.mean(values, axis=-1, keepdims=True))
    centered = values - average
    variance = lax.optimization_barrier(jnp.mean(centered * centered, axis=-1, keepdims=True))
    return centered * lax.rsqrt(variance + 1e-06)

def product(left, right, form):
    return jnp.einsum(form, left, right, precision=lax.Precision.HIGHEST)

def attention(joined):
    query_rows, key_rows, value_rows = (joined[:, 0], joined[:, 1], joined[:, 2])
    scores = low_back(product(query_rows, key_rows, 'qhe,khe->hqk') * 0.125)
    shares = low(jax.nn.softmax(scores, axis=-1))
    return product(shares, value_rows, 'hqk,khe->qhe')

def joint_block(streams, factors, attend_w, output_w, up_w, down_w):
    projected = []
    for stream in range(2):
        normed = low(layer_norm(streams[stream]) * (1.0 + factors[stream, 1]) + factors[stream, 0])
        projected.append(low_back(low(product(normed, attend_w[stream], 'ld,dcx->lcx'))))
    joined = jnp.concatenate(projected, axis=0).reshape(LEN, 3, HEADS, HD)
    mixture = low_back(low(attention(joined))).reshape(LEN, D)
    pieces = (mixture[:IMG], mixture[IMG:])
    results = []
    for stream in range(2):
        branch = low_back(product(pieces[stream], output_w[stream], 'lx,xd->ld'))
        middle = streams[stream] + factors[stream, 2] * branch
        normed = low(layer_norm(middle) * (1.0 + factors[stream, 4]) + factors[stream, 3])
        hidden_pre = low_back(product(normed, up_w[stream], 'ld,df->lf'))
        hidden_act = low(jax.nn.gelu(hidden_pre, approximate=True))
        feed_out = low_back(product(hidden_act, down_w[stream], 'lf,fd->ld'))
        results.append(middle + factors[stream, 5] * feed_out)
    return results

def forward(image, text, condition, attend_weight, output_weight, up_weight, down_weight, adaptive_weight):
    activated = low(jax.nn.silu(condition))
    modulation = low_back(product(activated, adaptive_weight, 'sd,bqdcx->bqscx'))
    per_sequence = jnp.moveaxis(modulation, 2, 0)

    def one_sequence(running, inputs):
        image_rows, text_rows, factors = inputs
        streams = [image_rows, text_rows]
        for block in range(BLOCKS):
            streams = joint_block(streams, factors[block], attend_weight[block], output_weight[block], up_weight[block], down_weight[block])
        return (running, (streams[0], streams[1]))
    initial = jnp.zeros((), jnp.float32)
    _, outputs = lax.scan(jax.checkpoint(one_sequence), initial, (image.reshape(SEQS, IMG, D), text.reshape(SEQS, TXT, D), per_sequence))
    return (outputs[0].reshape(SEQS * IMG, D), outputs[1].reshape(SEQS * TXT, D))

def reference(image, text, condition, attend_weight, output_weight, up_weight, down_weight, adaptive_weight, image_cotangent, text_cotangent):
    inputs = tuple((argument.astype(jnp.float32) for argument in (image, text, condition, attend_weight, output_weight, up_weight, down_weight, adaptive_weight)))
    outputs, pullback = jax.vjp(forward, *inputs)
    gradients = pullback((image_cotangent.astype(jnp.float32), text_cotangent.astype(jnp.float32)))
    return (outputs[0].astype(jnp.bfloat16), outputs[1].astype(jnp.bfloat16), gradients[0], gradients[1], gradients[2], gradients[3], gradients[4], gradients[5], gradients[6], gradients[7])
```

```python
import jax
import jax.numpy as jnp
from jax import lax
from jax.sharding import PartitionSpec as P

HD = 64
IMG = 870
TXT = 154
EPSILON = 1e-06


BF = jnp.bfloat16
F32 = jnp.float32


def ring_order(n):
    return [2 * p if p < n // 2 else 2 * (n - 1 - p) + 1 for p in range(n)]


def ring_place(index, n):
    return jnp.where(index % 2 == 0, index // 2, n - 1 - index // 2)


def ring_member(place, n):
    place = place % n
    return jnp.where(place < n // 2, 2 * place, 2 * (n - 1 - place) + 1)


class Layout:
    def __init__(self, width):
        self.n = lax.axis_size("gy")
        self.gx = lax.axis_size("gx")
        self.me = lax.axis_index("gy")
        self.mx = lax.axis_index("gx")
        self.place = ring_place(self.me, self.n)
        self.width = width
        self.rows = width * self.gx // self.n
        order = ring_order(self.n)
        self.cw = [(order[i], order[(i + 1) % self.n]) for i in range(self.n)]
        self.ccw = [(b, a) for a, b in self.cw]

    def offset(self, owner):
        per = self.width // self.rows
        relative = (owner // per) ^ self.mx
        swapped = (relative % 2) * 2 + relative // 2
        return swapped * self.width + (owner % per) * self.rows


def steps(lay, flip):
    far, near = lay.n // 2, lay.n - 1 - lay.n // 2
    return (near, far) if flip else (far, near)


def ring_gather(lay, shard, flip):
    n_cw, n_ccw = steps(lay, flip)
    pieces = [(shard, lay.me)]
    forward = backward = shard
    for k in range(1, max(n_cw, n_ccw) + 1):
        if k <= n_cw:
            forward = lax.ppermute(forward, "gy", lay.cw)
            pieces.append((forward, ring_member(lay.place - k + lay.n, lay.n)))
        if k <= n_ccw:
            backward = lax.ppermute(backward, "gy", lay.ccw)
            pieces.append((backward, ring_member(lay.place + k, lay.n)))
    return pieces


def assemble(lay, pieces):
    shape = pieces[0][0].shape
    full = jnp.zeros((shape[0], lay.rows * lay.n) + shape[2:], pieces[0][0].dtype)
    for piece, owner in pieces:
        full = lax.dynamic_update_slice_in_dim(full, piece, lay.offset(owner), 1)
    return full


def ring_scatter(lay, full, flip):
    n_cw, n_ccw = steps(lay, flip)

    def block(place):
        owner = ring_member(place + lay.n, lay.n)
        return lax.dynamic_slice_in_dim(full, lay.offset(owner), lay.rows, 1)

    forward = block(lay.place + n_cw)
    backward = block(lay.place - n_ccw)
    for k in range(max(n_cw, n_ccw), 0, -1):
        if k <= n_cw:
            got = lax.ppermute(forward, "gy", lay.cw)
            forward = got if k == 1 else (got.astype(F32) + block(lay.place + k - 1).astype(F32)).astype(BF)
        if k <= n_ccw:
            got = lax.ppermute(backward, "gy", lay.ccw)
            backward = got if k == 1 else (got.astype(F32) + block(lay.place - k + 1).astype(F32)).astype(BF)
    return block(lay.place).astype(F32) + forward.astype(F32) + backward.astype(F32)


def partner(lay, axis, bit):
    size = lay.gx if axis == "gx" else lay.n
    return [(i, i ^ bit) for i in range(size)]


def spread(lay, own):
    across = lax.ppermute(own, "gx", partner(lay, "gx", 2))
    beside = lax.ppermute(own, "gx", partner(lay, "gx", 1))
    beyond = lax.ppermute(across, "gx", partner(lay, "gx", 1))
    return jnp.concatenate([own, across, beside, beyond], axis=1)


def collect(lay, partial):
    w = lay.width
    got = lax.ppermute(partial[:, 2 * w :], "gx", partner(lay, "gx", 1))
    onward = (partial[:, w : 2 * w].astype(F32) + got[:, w:].astype(F32)).astype(BF)
    across = lax.ppermute(onward, "gx", partner(lay, "gx", 2))
    return partial[:, :w].astype(F32) + got[:, :w].astype(F32) + across.astype(F32)


def halve(lay, value, axis, index):
    size = value.shape[0]
    while size > 1:
        bit = size // 2
        value = value.reshape((2, bit) + value.shape[1:])
        side = (index // bit) % 2
        sent = lax.dynamic_index_in_dim(value, 1 - side, 0, keepdims=False)
        kept = lax.dynamic_index_in_dim(value, side, 0, keepdims=False)
        value = kept + lax.ppermute(sent, axis, partner(lay, axis, bit))
        size = bit
    return value


def double(lay, value, axis, index):
    size, bit = (lay.gx if axis == "gx" else lay.n), 1
    value = value[None]
    while bit < size:
        other = lax.ppermute(value, axis, partner(lay, axis, bit))
        side = (index // bit) % 2
        low = jnp.where(side == 0, value, other)
        high = jnp.where(side == 0, other, value)
        value = jnp.concatenate([low, high], axis=0)
        bit *= 2
    return value


def gelu_back(hidden_pre, upstream):
    _, pullback = jax.vjp(lambda argument: jax.nn.gelu(argument, approximate=True), hidden_pre)
    return pullback(upstream)[0]


def dual(x, weights, form):
    top = jnp.einsum(form, x[:IMG], weights[0], preferred_element_type=F32)
    low = jnp.einsum(form, x[IMG:], weights[1], preferred_element_type=F32)
    return top, low


def joint(pair):
    return jnp.concatenate(pair, axis=0)


def grads(left, right):
    return jnp.stack(
        [
            jnp.einsum("rk,rn->kn", left[:IMG], right[:IMG], preferred_element_type=F32).astype(BF),
            jnp.einsum("rk,rn->kn", left[IMG:], right[IMG:], preferred_element_type=F32).astype(BF),
        ]
    )


def attend_block(queries, key_rows, value_rows):
    scores = (
        jnp.einsum("qhe,khe->hqk", queries, key_rows, preferred_element_type=jnp.float32) * 0.125
    )
    highest = jnp.max(scores, axis=2, keepdims=True)
    weights = jnp.exp(scores - highest)
    totals = jnp.sum(weights, axis=2, keepdims=True)
    shares = (weights / totals).astype(jnp.bfloat16)
    mixture = jnp.einsum(
        "hqk,khe->qhe", shares, value_rows, preferred_element_type=jnp.float32
    ).astype(jnp.bfloat16)
    return (mixture, (highest + jnp.log(totals))[:, :, 0])


def attend_back(queries, key_rows, value_rows, logsum, upstream):
    scores = (
        jnp.einsum("qhe,khe->hqk", queries, key_rows, preferred_element_type=jnp.float32) * 0.125
    )
    shares = jnp.exp(scores - logsum[:, :, None])
    grad_shares = jnp.einsum(
        "qhe,khe->hqk", upstream, value_rows, preferred_element_type=jnp.float32
    )
    row_inner = jnp.sum(shares * grad_shares, axis=2, keepdims=True)
    grad_scores = (shares * (grad_shares - row_inner)).astype(jnp.bfloat16)
    grad_query = (
        jnp.einsum("hqk,khe->qhe", grad_scores, key_rows, preferred_element_type=jnp.float32)
        * 0.125
    )
    grad_key = (
        jnp.einsum("hqk,qhe->khe", grad_scores, queries, preferred_element_type=jnp.float32) * 0.125
    )
    grad_value = jnp.einsum(
        "hqk,qhe->khe", shares.astype(jnp.bfloat16), upstream, preferred_element_type=jnp.float32
    )
    return (grad_query, grad_key, grad_value)


def attend_sequence(projected):
    rows = projected.shape[0]
    joined = projected.reshape(rows, 3, -1, HD)
    q, k, v = joined[:, 0], joined[:, 1], joined[:, 2]
    half = rows // 2
    mixture, logsum = lax.map(
        lambda block: attend_block(block, k, v), q.reshape(2, half, q.shape[1], HD)
    )
    return mixture.reshape(rows, -1), logsum


def sequence_back(projected, logsum, upstream):
    rows = projected.shape[0]
    joined = projected.reshape(rows, 3, -1, HD)
    q, k, v = joined[:, 0], joined[:, 1], joined[:, 2]
    half = rows // 2
    q_blocks = q.reshape(2, half, q.shape[1], HD)
    up_blocks = upstream.reshape(2, half, q.shape[1], HD)

    def step(running, inputs):
        gq, gk, gv = attend_back(inputs[0], k, v, inputs[1], inputs[2])
        return (running[0] + gk, running[1] + gv), gq

    zero = jnp.zeros(k.shape, F32)
    (gk, gv), gq = lax.scan(step, (zero, zero), (q_blocks, logsum, up_blocks))
    return jnp.stack([gq.reshape(k.shape), gk, gv], axis=1).astype(BF).reshape(rows, -1)


def on_device(
    image,
    text,
    condition,
    attend_weight,
    output_weight,
    up_weight,
    down_weight,
    adaptive_weight,
    image_cotangent,
    text_cotangent,
):
    width = image.shape[1]
    rows = IMG + TXT
    lay = Layout(width)
    full_width = width * lay.gx
    is_image = (jnp.arange(rows) < IMG)[:, None]

    def per_row(pair):
        return jnp.where(is_image, pair[0][None, :], pair[1][None, :])

    def row_sums(value):
        top = jnp.sum(jnp.where(is_image, value, 0.0), axis=0)
        low = jnp.sum(jnp.where(is_image, 0.0, value), axis=0)
        return jnp.stack([top, low])

    attend_shard = attend_weight[0].reshape(2, lay.rows, 3 * width)
    output_shard = jnp.swapaxes(output_weight[0], 1, 2)
    up_shard = up_weight[0]
    down_shard = jnp.swapaxes(down_weight[0], 1, 2)
    attend_full = assemble(lay, ring_gather(lay, attend_shard, False))
    output_full = assemble(lay, ring_gather(lay, output_shard, True))
    up_full = assemble(lay, ring_gather(lay, up_shard, False))
    down_full = assemble(lay, ring_gather(lay, down_shard, True))

    activated = jax.nn.silu(condition.astype(F32)).astype(BF)
    partial_mod = jnp.einsum(
        "sd,qdcx->sqcx", activated, adaptive_weight[0], preferred_element_type=F32
    )
    factors = halve(lay, partial_mod, "gy", lay.me)[0]
    shift1, scale1, gate1, shift2, scale2, gate2 = [
        per_row(factors[:, k]) for k in range(6)
    ]

    def totals_of(first, second):
        totals = lax.psum(jnp.stack([jnp.sum(first, axis=1), jnp.sum(second, axis=1)]), "gx")
        return totals[0][:, None] / full_width, totals[1][:, None] / full_width

    def normalize(value, shift, scale):
        average, square = totals_of(value, value * value)
        inverse = lax.rsqrt(square - average * average + EPSILON)
        unit = (value - average) * inverse
        lowered = (unit * (1.0 + scale) + shift).astype(BF)
        return unit, inverse, spread(lay, lowered)

    def norm_back(grad, unit, inverse, scale):
        scaled = grad * (1.0 + scale)
        mean, inner = totals_of(scaled, scaled * unit)
        result = inverse * (scaled - mean - unit * inner)
        return result, row_sums(grad * unit), row_sums(grad)

    stream = jnp.concatenate([image, text], axis=0).astype(F32)
    cotangent = jnp.concatenate([image_cotangent, text_cotangent], axis=0).astype(F32)

    unit1, inverse1, first_full = normalize(stream, shift1, scale1)
    feed_full = spread(lay, (gate2 * cotangent).astype(BF))
    projected = joint(dual(first_full, attend_full, "rk,kn->rn")).astype(BF)
    mixture, logsum = attend_sequence(projected)
    branch = collect(lay, joint(dual(mixture, output_full, "rk,nk->rn")).astype(BF))
    middle = stream + gate1 * branch
    unit2, inverse2, second_full = normalize(middle, shift2, scale2)
    hidden = joint(dual(second_full, up_full, "rk,kn->rn"))
    active = jax.nn.gelu(hidden, approximate=True).astype(BF)
    down_grad = ring_scatter(lay, grads(feed_full, active), False)
    feed = collect(lay, joint(dual(active, down_full, "rk,nk->rn")).astype(BF))
    result = middle + gate2 * feed
    gate2_grad = row_sums(cotangent * feed)

    active_grad = joint(dual(feed_full, down_full, "rk,kn->rn"))
    hidden_grad = gelu_back(hidden, active_grad).astype(BF)
    up_grad = ring_scatter(lay, grads(second_full, hidden_grad), True)
    second_grad = collect(lay, joint(dual(hidden_grad, up_full, "rk,nk->rn")).astype(BF))
    middle_part, scale2_grad, shift2_grad = norm_back(second_grad, unit2, inverse2, scale2)
    middle_grad = cotangent + middle_part
    gate1_grad = row_sums(middle_grad * branch)
    branch_full = spread(lay, (gate1 * middle_grad).astype(BF))
    mixed_grad = joint(dual(branch_full, output_full, "rk,kn->rn")).astype(BF)
    output_grad = ring_scatter(lay, grads(branch_full, mixture), False)
    projected_grad = sequence_back(projected, logsum, mixed_grad)
    attend_grad = ring_scatter(lay, grads(first_full, projected_grad), True)
    first_grad = collect(lay, joint(dual(projected_grad, attend_full, "rk,nk->rn")).astype(BF))
    input_part, scale1_grad, shift1_grad = norm_back(first_grad, unit1, inverse1, scale1)
    input_grad = middle_grad + input_part

    modulation_grad = jnp.stack(
        [shift1_grad, scale1_grad, gate1_grad, shift2_grad, scale2_grad, gate2_grad], axis=1
    ).astype(BF)
    all_mod = double(lay, modulation_grad, "gy", lay.me)
    adaptive_grad = jnp.einsum("sd,sqcx->qdcx", activated, all_mod, preferred_element_type=F32)
    condition_partial = jnp.einsum(
        "sqcx,qdcx->sd", all_mod, adaptive_weight[0], preferred_element_type=F32
    )
    share_rows = condition.shape[0] // lay.gx
    condition_share = halve(
        lay, condition_partial.reshape(lay.gx, share_rows, -1), "gx", lay.mx
    )[0]
    own_condition = lax.dynamic_slice_in_dim(condition, lay.mx * share_rows, share_rows, 0)
    _, silu_pullback = jax.vjp(jax.nn.silu, own_condition.astype(F32))
    condition_grad = silu_pullback(condition_share)[0]
    return (
        result[:IMG].astype(BF),
        result[IMG:].astype(BF),
        input_grad[:IMG],
        input_grad[IMG:],
        condition_grad,
        attend_grad.reshape((1,) + attend_weight.shape[1:]),
        jnp.swapaxes(output_grad, 1, 2)[None],
        up_grad[None],
        jnp.swapaxes(down_grad, 1, 2)[None],
        adaptive_grad[None],
    )


def solution(mesh):
    placed = (
        P("gy", "gx"),
        P("gy", "gx"),
        P(None, "gy"),
        P(None, None, "gy", None, "gx"),
        P(None, None, "gx", "gy"),
        P(None, None, "gy", "gx"),
        P(None, None, "gx", "gy"),
        P(None, None, "gy", None, "gx"),
        P("gy", "gx"),
        P("gy", "gx"),
    )
    return jax.shard_map(
        on_device,
        mesh=mesh,
        in_specs=placed,
        out_specs=(
            P("gy", "gx"),
            P("gy", "gx"),
            P("gy", "gx"),
            P("gy", "gx"),
            P("gx", "gy"),
            P(None, None, "gy", None, "gx"),
            P(None, None, "gx", "gy"),
            P(None, None, "gy", "gx"),
            P(None, None, "gx", "gy"),
            P(None, None, "gy", None, "gx"),
        ),
        check_vma=False,
    )
```

```python
import functools

import jax
import jax.numpy as jnp
from jax import lax
from jax.experimental import pallas as pl
from jax.experimental.pallas import tpu as pltpu
from jax.sharding import PartitionSpec as P

HD = 64
IMG = 870
TXT = 154
EPSILON = 1e-06


BF = jnp.bfloat16
F32 = jnp.float32


def ring_order(n):
    return [2 * p if p < n // 2 else 2 * (n - 1 - p) + 1 for p in range(n)]


def ring_place(index, n):
    return jnp.where(index % 2 == 0, index // 2, n - 1 - index // 2)


def ring_member(place, n):
    place = place % n
    return jnp.where(place < n // 2, 2 * place, 2 * (n - 1 - place) + 1)


class Layout:
    def __init__(self, width):
        self.n = lax.axis_size("gy")
        self.gx = lax.axis_size("gx")
        self.me = lax.axis_index("gy")
        self.mx = lax.axis_index("gx")
        self.place = ring_place(self.me, self.n)
        self.width = width
        self.rows = width * self.gx // self.n
        order = ring_order(self.n)
        self.cw = [(order[i], order[(i + 1) % self.n]) for i in range(self.n)]
        self.ccw = [(b, a) for a, b in self.cw]

    def offset(self, owner):
        per = self.width // self.rows
        relative = (owner // per) ^ self.mx
        swapped = (relative % 2) * 2 + relative // 2
        return swapped * self.width + (owner % per) * self.rows


def steps(lay, flip):
    far, near = lay.n // 2, lay.n - 1 - lay.n // 2
    return (near, far) if flip else (far, near)


def ring_gather(lay, shard, flip):
    n_cw, n_ccw = steps(lay, flip)
    pieces = [(shard, lay.me)]
    forward = backward = shard
    for k in range(1, max(n_cw, n_ccw) + 1):
        if k <= n_cw:
            forward = lax.ppermute(forward, "gy", lay.cw)
            pieces.append((forward, ring_member(lay.place - k + lay.n, lay.n)))
        if k <= n_ccw:
            backward = lax.ppermute(backward, "gy", lay.ccw)
            pieces.append((backward, ring_member(lay.place + k, lay.n)))
    return pieces


def ring_scatter(lay, full, flip):
    n_cw, n_ccw = steps(lay, flip)

    def block(place):
        owner = ring_member(place + lay.n, lay.n)
        return lax.dynamic_slice_in_dim(full, lay.offset(owner), lay.rows, 1)

    forward = block(lay.place + n_cw)
    backward = block(lay.place - n_ccw)
    for k in range(max(n_cw, n_ccw), 0, -1):
        if k <= n_cw:
            got = lax.ppermute(forward, "gy", lay.cw)
            forward = got if k == 1 else (got.astype(F32) + block(lay.place + k - 1).astype(F32)).astype(BF)
        if k <= n_ccw:
            got = lax.ppermute(backward, "gy", lay.ccw)
            backward = got if k == 1 else (got.astype(F32) + block(lay.place - k + 1).astype(F32)).astype(BF)
    return block(lay.place).astype(F32) + forward.astype(F32) + backward.astype(F32)


def partner(lay, axis, bit):
    size = lay.gx if axis == "gx" else lay.n
    return [(i, i ^ bit) for i in range(size)]


def spread(lay, own):
    across = lax.ppermute(own, "gx", partner(lay, "gx", 2))
    beside = lax.ppermute(own, "gx", partner(lay, "gx", 1))
    beyond = lax.ppermute(across, "gx", partner(lay, "gx", 1))
    return [own, across, beside, beyond]


def collect(lay, kept, sent):
    w = lay.width
    got = lax.ppermute(sent, "gx", partner(lay, "gx", 1))
    onward = (kept[:, w:].astype(F32) + got[:, w:].astype(F32)).astype(BF)
    across = lax.ppermute(onward, "gx", partner(lay, "gx", 2))
    return kept[:, :w].astype(F32) + got[:, :w].astype(F32) + across.astype(F32)


def halve(lay, value, axis, index):
    size = value.shape[0]
    while size > 1:
        bit = size // 2
        value = value.reshape((2, bit) + value.shape[1:])
        side = (index // bit) % 2
        sent = lax.dynamic_index_in_dim(value, 1 - side, 0, keepdims=False)
        kept = lax.dynamic_index_in_dim(value, side, 0, keepdims=False)
        value = kept + lax.ppermute(sent, axis, partner(lay, axis, bit))
        size = bit
    return value


def double(lay, value, axis, index):
    size, bit = (lay.gx if axis == "gx" else lay.n), 1
    value = value[None]
    while bit < size:
        other = lax.ppermute(value, axis, partner(lay, axis, bit))
        side = (index // bit) % 2
        low = jnp.where(side == 0, value, other)
        high = jnp.where(side == 0, other, value)
        value = jnp.concatenate([low, high], axis=0)
        bit *= 2
    return value


ROOT = 0.7978845608028654
CUBE = 0.044715
LO = IMG // 16 * 16
HI = (IMG + 15) // 16 * 16


def gelu(hidden):
    return 0.5 * hidden * (1.0 + jnp.tanh(ROOT * (hidden + CUBE * (hidden * hidden * hidden))))


def gelu_slope(hidden):
    square = hidden * hidden
    curve = jnp.tanh(ROOT * (hidden + CUBE * (square * hidden)))
    return 0.5 * (1.0 + curve) + 0.5 * hidden * (1.0 - curve * curve) * (
        ROOT * (1.0 + 3.0 * CUBE * square)
    )


def is_image_rows(count):
    return LO + lax.broadcasted_iota(jnp.int32, (HI - LO, count), 0) < IMG


def place_columns(sources, target, sems):
    copies, at = [], 0
    for k, source in enumerate(sources):
        size = source.shape[1]
        copies.append(pltpu.make_async_copy(source, target.at[:, at : at + size], sems.at[k]))
        at += size
    return copies


def store_rows(store, top, low):
    edge = jnp.where(is_image_rows(top.shape[1]), top[LO:HI], low[: HI - LO])
    store(slice(0, LO), top[:LO])
    store(slice(LO, HI), edge)
    store(slice(HI, None), low[HI - LO :])


ANY = pl.BlockSpec(memory_space=pl.ANY)


def forward_kernel(nx, npieces, nextra, tile, finish, offsets, *refs):
    xs, pieces = refs[:nx], refs[nx : nx + npieces]
    extras = refs[nx + npieces : nx + npieces + nextra]
    outs = refs[nx + npieces + nextra : -4]
    xbuf, wbuf, xsem, wsem = refs[-4:]
    step, total = pl.program_id(0), pl.num_programs(0)
    slot = lax.rem(step, 2)

    def weight_copies(index, slot):
        columns = pl.ds(pl.multiple_of(index * tile, tile), tile)
        return [
            pltpu.make_async_copy(
                piece.at[:, :, columns],
                wbuf.at[slot, :, pl.ds(pl.multiple_of(offsets[k], 16), piece.shape[1]), :],
                wsem.at[slot, k],
            )
            for k, piece in enumerate(pieces)
        ]

    @pl.when(step == 0)
    def _():
        for copy in place_columns(xs, xbuf, xsem):
            copy.start()
        for copy in weight_copies(0, 0):
            copy.start()

    @pl.when(step + 1 < total)
    def _():
        for copy in weight_copies(step + 1, 1 - slot):
            copy.start()

    @pl.when(step == 0)
    def _():
        for copy in place_columns(xs, xbuf, xsem):
            copy.wait()

    for copy in weight_copies(step, slot):
        copy.wait()
    top = jnp.dot(xbuf[:HI], wbuf[slot, 0], preferred_element_type=F32)
    low = jnp.dot(xbuf[LO:], wbuf[slot, 1], preferred_element_type=F32)
    store_rows(lambda where, value: finish(where, value, extras, outs), top, low)


def plain_finish(where, value, extras, outs):
    outs[0][where, :] = value.astype(outs[0].dtype)


def gelu_finish(where, value, extras, outs):
    outs[0][where, :] = value
    outs[1][where, :] = gelu(value).astype(BF)


def slope_finish(where, value, extras, outs):
    outs[0][where, :] = (gelu_slope(extras[0][where, :]) * value).astype(BF)


def forward_product(lay, xs, pieces, tile, finish, out_types, extras=()):
    rows = xs[0].shape[0]
    depth = sum(x.shape[1] for x in xs)
    columns = pieces[0][0].shape[2]
    offsets = jnp.stack([lay.offset(owner) for _, owner in pieces]).astype(jnp.int32)
    block = pl.BlockSpec((rows, tile), lambda i, _: (0, i))
    return pl.pallas_call(
        functools.partial(forward_kernel, len(xs), len(pieces), len(extras), tile, finish),
        grid_spec=pltpu.PrefetchScalarGridSpec(
            num_scalar_prefetch=1,
            grid=(columns // tile,),
            in_specs=[ANY] * (len(xs) + len(pieces)) + [block] * len(extras),
            out_specs=[block] * len(out_types),
            scratch_shapes=[
                pltpu.VMEM((rows, depth), BF),
                pltpu.VMEM((2, 2, depth, tile), BF),
                pltpu.SemaphoreType.DMA((len(xs),)),
                pltpu.SemaphoreType.DMA((2, len(pieces))),
            ],
        ),
        out_shape=[jax.ShapeDtypeStruct((rows, columns), dtype) for dtype in out_types],
        cost_estimate=pl.CostEstimate(
            flops=2 * rows * depth * columns,
            bytes_accessed=2 * (rows * depth + 2 * depth * columns + rows * columns),
            transcendentals=0,
        ),
    )(offsets, *xs, *[piece for piece, _ in pieces], *extras)


def backward_kernel(nx, npieces, tile, offsets, *refs):
    xs, pieces = refs[:nx], refs[nx : nx + npieces]
    kept, sent = refs[nx + npieces : nx + npieces + 2]
    xbuf, wbuf, xsem, wsem = refs[-4:]
    step, total = pl.program_id(0), pl.num_programs(0)
    half = total // 2

    def weight_copies(stream):
        return [
            pltpu.make_async_copy(
                piece.at[stream],
                wbuf.at[stream, pl.ds(pl.multiple_of(offsets[k], 16), piece.shape[1]), :],
                wsem.at[stream, k],
            )
            for k, piece in enumerate(pieces)
        ]

    @pl.when(step == 0)
    def _():
        for copy in place_columns(xs, xbuf, xsem) + weight_copies(0) + weight_copies(1):
            copy.start()
        for copy in place_columns(xs, xbuf, xsem) + weight_copies(0) + weight_copies(1):
            copy.wait()

    window = pl.ds(pl.multiple_of(lax.rem(step + half, total) * tile, tile), tile)
    dims = (((1,), (1,)), ((), ()))
    top = lax.dot_general(xbuf[:HI], wbuf[0, window, :], dims, preferred_element_type=F32)
    low = lax.dot_general(xbuf[LO:], wbuf[1, window, :], dims, preferred_element_type=F32)

    def write(out):
        def store(where, value):
            out[where, :] = value.astype(BF)

        store_rows(store, top, low)

    @pl.when(step < half)
    def _():
        write(sent)

    @pl.when(step >= half)
    def _():
        write(kept)


def backward_product(lay, xs, pieces, tile):
    rows = xs[0].shape[0]
    depth = sum(x.shape[1] for x in xs)
    columns = lay.width * lay.gx
    offsets = jnp.stack([lay.offset(owner) for _, owner in pieces]).astype(jnp.int32)
    total = columns // tile
    half = total // 2
    return pl.pallas_call(
        functools.partial(backward_kernel, len(xs), len(pieces), tile),
        grid_spec=pltpu.PrefetchScalarGridSpec(
            num_scalar_prefetch=1,
            grid=(total,),
            in_specs=[ANY] * (len(xs) + len(pieces)),
            out_specs=[
                pl.BlockSpec((rows, tile), lambda i, _: (0, jnp.maximum(i - half, 0))),
                pl.BlockSpec((rows, tile), lambda i, _: (0, jnp.minimum(i, half - 1))),
            ],
            scratch_shapes=[
                pltpu.VMEM((rows, depth), BF),
                pltpu.VMEM((2, columns, depth), BF),
                pltpu.SemaphoreType.DMA((len(xs),)),
                pltpu.SemaphoreType.DMA((2, len(pieces))),
            ],
        ),
        out_shape=[jax.ShapeDtypeStruct((rows, columns // 2), BF)] * 2,
        cost_estimate=pl.CostEstimate(
            flops=2 * rows * depth * columns,
            bytes_accessed=2 * (rows * depth + 2 * depth * columns + rows * columns),
            transcendentals=0,
        ),
    )(offsets, *xs, *[piece for piece, _ in pieces])


def weight_kernel(nleft, nright, *refs):
    lefts, rights = refs[:nleft], refs[nleft : nleft + nright]
    out = refs[nleft + nright]
    lbuf, rbuf, lsem, rsem = refs[-4:]
    step = pl.program_id(0)

    def left_copies():
        return [
            pltpu.make_async_copy(left, lbuf.at[k], lsem.at[k]) for k, left in enumerate(lefts)
        ]

    @pl.when(step == 0)
    def _():
        for copy in place_columns(rights, rbuf, rsem) + left_copies():
            copy.start()
        for copy in place_columns(rights, rbuf, rsem) + left_copies():
            copy.wait()

    block = lbuf[step]
    edge = block[LO:HI]
    image = is_image_rows(edge.shape[1])
    zero = jnp.zeros_like(edge)
    top = jnp.concatenate([block[:LO], jnp.where(image, edge, zero)], axis=0)
    low = jnp.concatenate([jnp.where(image, zero, edge), block[HI:]], axis=0)
    dims = (((0,), (0,)), ((), ()))
    out[0] = lax.dot_general(top, rbuf[:HI], dims, preferred_element_type=F32).astype(BF)
    out[1] = lax.dot_general(low, rbuf[LO:], dims, preferred_element_type=F32).astype(BF)


def weight_product(lay, lefts, rights):
    rows, width = lefts[0].shape
    depth = width * len(lefts)
    columns = sum(right.shape[1] for right in rights)
    return pl.pallas_call(
        functools.partial(weight_kernel, len(lefts), len(rights)),
        grid=(len(lefts),),
        in_specs=[ANY] * (len(lefts) + len(rights)),
        out_specs=pl.BlockSpec((2, width, columns), lambda i: (0, i, 0)),
        scratch_shapes=[
            pltpu.VMEM((len(lefts), rows, width), BF),
            pltpu.VMEM((rows, columns), BF),
            pltpu.SemaphoreType.DMA((len(lefts),)),
            pltpu.SemaphoreType.DMA((len(rights),)),
        ],
        out_shape=jax.ShapeDtypeStruct((2, depth, columns), BF),
        cost_estimate=pl.CostEstimate(
            flops=2 * rows * depth * columns,
            bytes_accessed=2 * (rows * depth + 2 * depth * columns + rows * columns),
            transcendentals=0,
        ),
    )(*lefts, *rights)


ACROSS = (((1,), (1,)), ((), ()))
DOWN = (((0,), (0,)), ((), ()))
PLAIN = (((1,), (0,)), ((), ()))


def only_head(block, head):
    lane = lax.broadcasted_iota(jnp.int32, block.shape, 1)
    return jnp.where(lane // HD == head, block, jnp.zeros_like(block))


def attend_kernel(q_ref, k_ref, v_ref, mix_ref, log_ref, turned):
    @pl.when(pl.program_id(1) == 0)
    def _():
        turned[...] = v_ref[...].T

    halves = []
    for head in range(2):
        query = only_head(q_ref[...], head)
        scores = lax.dot_general(k_ref[...], query, ACROSS, preferred_element_type=F32) * 0.125
        highest = jnp.max(scores, axis=0, keepdims=True)
        powers = jnp.exp(scores - highest)
        total = jnp.sum(powers, axis=0, keepdims=True)
        shares = (powers * (1.0 / total)).astype(BF)
        values = turned[head * HD : (head + 1) * HD, :]
        halves.append(lax.dot_general(values, shares, PLAIN, preferred_element_type=F32))
        log_ref[0, head : head + 1, :] = highest + jnp.log(total)
    mix_ref[...] = jnp.concatenate(halves, axis=0).T.astype(BF)


def attention(projected, chunk):
    rows, columns = projected.shape
    width = columns // 3
    pairs = width // (2 * HD)
    lanes = 2 * HD
    return pl.pallas_call(
        attend_kernel,
        grid=(pairs, rows // chunk),
        in_specs=[
            pl.BlockSpec((chunk, lanes), lambda p, i: (i, p)),
            pl.BlockSpec((rows, lanes), lambda p, i: (0, pairs + p)),
            pl.BlockSpec((rows, lanes), lambda p, i: (0, 2 * pairs + p)),
        ],
        out_specs=[
            pl.BlockSpec((chunk, lanes), lambda p, i: (i, p)),
            pl.BlockSpec((1, 2, chunk), lambda p, i: (p, 0, i)),
        ],
        scratch_shapes=[pltpu.VMEM((lanes, rows), BF)],
        out_shape=[
            jax.ShapeDtypeStruct((rows, width), BF),
            jax.ShapeDtypeStruct((pairs, 2, rows), F32),
        ],
        cost_estimate=pl.CostEstimate(
            flops=16 * rows * rows * width, bytes_accessed=8 * rows * width, transcendentals=0
        ),
    )(projected, projected, projected)


def attend_back_kernel(
    q_ref, k_ref, v_ref, log_ref, up_ref, dq_ref, dk_ref, dv_ref, turned, key_sum, value_sum
):
    step = pl.program_id(1)

    @pl.when(step == 0)
    def _():
        turned[...] = k_ref[...].T
        key_sum[...] = jnp.zeros_like(key_sum)
        value_sum[...] = jnp.zeros_like(value_sum)

    halves = []
    for head in range(2):
        query = only_head(q_ref[...], head)
        upstream = only_head(up_ref[...], head)
        scores = lax.dot_general(k_ref[...], query, ACROSS, preferred_element_type=F32) * 0.125
        shares = jnp.exp(scores - log_ref[0, head : head + 1, :])
        value_sum[...] += lax.dot_general(
            shares.astype(BF), upstream, PLAIN, preferred_element_type=F32
        )
        slope = lax.dot_general(v_ref[...], upstream, ACROSS, preferred_element_type=F32)
        inner = jnp.sum(shares * slope, axis=0, keepdims=True)
        score_grad = (shares * (slope - inner)).astype(BF)
        key_sum[...] += lax.dot_general(score_grad, query, PLAIN, preferred_element_type=F32)
        keys = turned[head * HD : (head + 1) * HD, :]
        halves.append(lax.dot_general(keys, score_grad, PLAIN, preferred_element_type=F32))
    dq_ref[...] = (jnp.concatenate(halves, axis=0).T * 0.125).astype(BF)

    @pl.when(step == pl.num_programs(1) - 1)
    def _():
        dk_ref[...] = (key_sum[...] * 0.125).astype(BF)
        dv_ref[...] = value_sum[...].astype(BF)


def attention_back(projected, logsum, upstream, chunk):
    rows, columns = projected.shape
    width = columns // 3
    pairs = width // (2 * HD)
    lanes = 2 * HD
    part = pl.BlockSpec((chunk, lanes), lambda p, i: (i, p))
    whole = pl.BlockSpec((rows, lanes), lambda p, i: (0, p))
    return pl.pallas_call(
        attend_back_kernel,
        grid=(pairs, rows // chunk),
        in_specs=[
            part,
            pl.BlockSpec((rows, lanes), lambda p, i: (0, pairs + p)),
            pl.BlockSpec((rows, lanes), lambda p, i: (0, 2 * pairs + p)),
            pl.BlockSpec((1, 2, chunk), lambda p, i: (p, 0, i)),
            part,
        ],
        out_specs=[part, whole, whole],
        scratch_shapes=[
            pltpu.VMEM((lanes, rows), BF),
            pltpu.VMEM((rows, lanes), F32),
            pltpu.VMEM((rows, lanes), F32),
        ],
        out_shape=[jax.ShapeDtypeStruct((rows, width), BF)] * 3,
        cost_estimate=pl.CostEstimate(
            flops=40 * rows * rows * width, bytes_accessed=16 * rows * width, transcendentals=0
        ),
    )(projected, projected, projected, logsum, upstream)


def after(value, *others):
    return lax.optimization_barrier((value,) + others)[0]


def on_device(
    image,
    text,
    condition,
    attend_weight,
    output_weight,
    up_weight,
    down_weight,
    adaptive_weight,
    image_cotangent,
    text_cotangent,
):
    width = image.shape[1]
    rows = IMG + TXT
    lay = Layout(width)
    full_width = width * lay.gx
    is_image = (jnp.arange(rows) < IMG)[:, None]

    def per_row(pair):
        return jnp.where(is_image, pair[0][None, :], pair[1][None, :])

    def row_sums(value):
        top = jnp.sum(jnp.where(is_image, value, 0.0), axis=0)
        low = jnp.sum(jnp.where(is_image, 0.0, value), axis=0)
        return jnp.stack([top, low])

    activated = jax.nn.silu(condition.astype(F32)).astype(BF)
    partial_mod = jnp.einsum(
        "sd,qdcx->sqcx", activated, adaptive_weight[0], preferred_element_type=F32
    )
    factors = halve(lay, partial_mod, "gy", lay.me)[0]
    attend_shard = attend_weight[0].reshape(2, lay.rows, 3 * width)
    output_shard = jnp.swapaxes(output_weight[0], 1, 2)
    down_shard = jnp.swapaxes(down_weight[0], 1, 2)
    attend_pieces = ring_gather(lay, after(attend_shard, factors), False)
    output_pieces = ring_gather(lay, after(output_shard, attend_pieces[5][0]), True)
    up_pieces = ring_gather(lay, after(up_weight[0], output_pieces[5][0]), False)
    down_pieces = ring_gather(lay, after(down_shard, up_pieces[5][0]), True)

    shift1, scale1, gate1, shift2, scale2, gate2 = [
        per_row(factors[:, k]) for k in range(6)
    ]

    def totals_of(first, second):
        totals = lax.psum(jnp.stack([jnp.sum(first, axis=1), jnp.sum(second, axis=1)]), "gx")
        return totals[0][:, None] / full_width, totals[1][:, None] / full_width

    def normalize(value, shift, scale):
        average, square = totals_of(value, value * value)
        inverse = lax.rsqrt(square - average * average + EPSILON)
        unit = (value - average) * inverse
        lowered = (unit * (1.0 + scale) + shift).astype(BF)
        return unit, inverse, spread(lay, lowered)

    def norm_back(grad, unit, inverse, scale):
        scaled = grad * (1.0 + scale)
        mean, inner = totals_of(scaled, scaled * unit)
        result = inverse * (scaled - mean - unit * inner)
        return result, row_sums(grad * unit), row_sums(grad)

    stream = jnp.concatenate([image, text], axis=0).astype(F32)
    cotangent = jnp.concatenate([image_cotangent, text_cotangent], axis=0).astype(F32)

    unit1, inverse1, first_full = normalize(stream, shift1, scale1)
    feed_full = spread(lay, (gate2 * cotangent).astype(BF))
    projected = forward_product(lay, first_full, attend_pieces, width, plain_finish, [BF])[0]
    mixture, logsum = attention(projected, 256)
    branch = collect(lay, *backward_product(lay, [mixture], output_pieces, width))
    middle = stream + gate1 * branch
    unit2, inverse2, second_full = normalize(middle, shift2, scale2)
    hidden, active = forward_product(lay, second_full, up_pieces, 256, gelu_finish, [F32, BF])
    down_grad = ring_scatter(lay, weight_product(lay, feed_full, [active]), False)
    feed = collect(lay, *backward_product(lay, [active], down_pieces, width))
    result = middle + gate2 * feed
    gate2_grad = row_sums(cotangent * feed)

    hidden_grad = forward_product(
        lay, feed_full, down_pieces, 256, slope_finish, [BF], [hidden]
    )[0]
    up_grad = ring_scatter(lay, weight_product(lay, second_full, [hidden_grad]), True)
    second_grad = collect(lay, *backward_product(lay, [hidden_grad], up_pieces, width))
    middle_part, scale2_grad, shift2_grad = norm_back(second_grad, unit2, inverse2, scale2)
    middle_grad = cotangent + middle_part
    gate1_grad = row_sums(middle_grad * branch)
    branch_full = spread(lay, (gate1 * middle_grad).astype(BF))
    mixed_grad = forward_product(lay, branch_full, output_pieces, width, plain_finish, [BF])[0]
    output_grad = ring_scatter(lay, weight_product(lay, branch_full, [mixture]), False)
    projected_grad = attention_back(projected, logsum, mixed_grad, 256)
    attend_grad = ring_scatter(lay, weight_product(lay, first_full, projected_grad), True)
    first_grad = collect(lay, *backward_product(lay, projected_grad, attend_pieces, width))
    input_part, scale1_grad, shift1_grad = norm_back(first_grad, unit1, inverse1, scale1)
    input_grad = middle_grad + input_part

    modulation_grad = jnp.stack(
        [shift1_grad, scale1_grad, gate1_grad, shift2_grad, scale2_grad, gate2_grad], axis=1
    ).astype(BF)
    all_mod = double(lay, modulation_grad, "gy", lay.me)
    adaptive_grad = jnp.einsum("sd,sqcx->qdcx", activated, all_mod, preferred_element_type=F32)
    condition_partial = jnp.einsum(
        "sqcx,qdcx->sd", all_mod, adaptive_weight[0], preferred_element_type=F32
    )
    share_rows = condition.shape[0] // lay.gx
    condition_share = halve(
        lay, condition_partial.reshape(lay.gx, share_rows, -1), "gx", lay.mx
    )[0]
    own_condition = lax.dynamic_slice_in_dim(condition, lay.mx * share_rows, share_rows, 0)
    _, silu_pullback = jax.vjp(jax.nn.silu, own_condition.astype(F32))
    condition_grad = silu_pullback(condition_share)[0]
    return (
        result[:IMG].astype(BF),
        result[IMG:].astype(BF),
        input_grad[:IMG],
        input_grad[IMG:],
        condition_grad,
        attend_grad.reshape((1,) + attend_weight.shape[1:]),
        jnp.swapaxes(output_grad, 1, 2)[None],
        up_grad[None],
        jnp.swapaxes(down_grad, 1, 2)[None],
        adaptive_grad[None],
    )


def solution(mesh):
    placed = (
        P("gy", "gx"),
        P("gy", "gx"),
        P(None, "gy"),
        P(None, None, "gy", None, "gx"),
        P(None, None, "gx", "gy"),
        P(None, None, "gy", "gx"),
        P(None, None, "gx", "gy"),
        P(None, None, "gy", None, "gx"),
        P("gy", "gx"),
        P("gy", "gx"),
    )
    return jax.shard_map(
        on_device,
        mesh=mesh,
        in_specs=placed,
        out_specs=(
            P("gy", "gx"),
            P("gy", "gx"),
            P("gy", "gx"),
            P("gy", "gx"),
            P("gx", "gy"),
            P(None, None, "gy", None, "gx"),
            P(None, None, "gx", "gy"),
            P(None, None, "gy", "gx"),
            P(None, None, "gx", "gy"),
            P(None, None, "gy", None, "gx"),
        ),
        check_vma=False,
    )
```

```python
import functools

import jax
import jax.numpy as jnp
from jax import lax
from jax.experimental import pallas as pl
from jax.experimental.pallas import tpu as pltpu
from jax.sharding import PartitionSpec as P


HD = 64
IMG = 870
TXT = 154
EPSILON = 1e-06


BF = jnp.bfloat16
F32 = jnp.float32


def ring_order(n):
    return [2 * p if p < n // 2 else 2 * (n - 1 - p) + 1 for p in range(n)]


def ring_place(index, n):
    return jnp.where(index % 2 == 0, index // 2, n - 1 - index // 2)


def ring_member(place, n):
    place = place % n
    return jnp.where(place < n // 2, 2 * place, 2 * (n - 1 - place) + 1)


class Layout:
    def __init__(self, width):
        self.n = lax.axis_size("gy")
        self.gx = lax.axis_size("gx")
        self.me = lax.axis_index("gy")
        self.mx = lax.axis_index("gx")
        self.place = ring_place(self.me, self.n)
        self.width = width
        self.rows = width * self.gx // self.n
        order = ring_order(self.n)
        self.cw = [(order[i], order[(i + 1) % self.n]) for i in range(self.n)]
        self.ccw = [(b, a) for a, b in self.cw]

    def offset(self, owner):
        per = self.width // self.rows
        relative = (owner // per) ^ self.mx
        swapped = (relative % 2) * 2 + relative // 2
        return swapped * self.width + (owner % per) * self.rows


class Gathered:
    def __init__(self, arrays, runs):
        self.arrays, self.runs = arrays, runs

    def offsets(self, lay):
        return jnp.stack(
            [lay.offset(owner) + inner for _, _, _, _, owner, inner in self.runs]
        ).astype(jnp.int32)


def first_half(rows):
    return (rows // 2 + 15) // 16 * 16


def ring_gather(lay, shard):
    rows, far = lay.rows, lay.n // 2
    half = first_half(rows)
    arrays, runs = [shard], [(0, (), 0, rows, lay.me, 0)]
    forward = backward = shard
    for k in range(1, far):
        forward = lax.ppermute(forward, "gy", lay.cw)
        backward = lax.ppermute(backward, "gy", lay.ccw)
        runs.append((len(arrays), (), 0, rows, ring_member(lay.place - k + lay.n, lay.n), 0))
        runs.append((len(arrays) + 1, (), 0, rows, ring_member(lay.place + k, lay.n), 0))
        arrays += [forward, backward]
    last = ring_member(lay.place + far, lay.n)
    runs.append((len(arrays), (), 0, half, last, 0))
    runs.append((len(arrays) + 1, (), 0, rows - half, last, half))
    arrays.append(lax.ppermute(forward[:, :half], "gy", lay.cw))
    arrays.append(lax.ppermute(backward[:, half:], "gy", lay.ccw))
    return Gathered(arrays, runs)


def ring_scatter(lay, full):
    rows, far = lay.rows, lay.n // 2
    half = first_half(rows)

    def block(place):
        owner = ring_member(place + lay.n, lay.n)
        return lax.dynamic_index_in_dim(full, owner, 0, keepdims=False)

    def plus(got, own):
        return (got.astype(F32) + own.astype(F32)).astype(BF)

    last = block(lay.place + far)
    forward = lax.ppermute(last[:, :half], "gy", lay.cw)
    backward = lax.ppermute(last[:, half:], "gy", lay.ccw)
    for k in range(far - 1, 0, -1):
        ahead, behind = block(lay.place + k), block(lay.place - k)
        if k == far - 1:
            ahead = jnp.concatenate([plus(forward, ahead[:, :half]), ahead[:, half:]], axis=1)
            behind = jnp.concatenate([behind[:, :half], plus(backward, behind[:, half:])], axis=1)
        else:
            ahead, behind = plus(forward, ahead), plus(backward, behind)
        forward = lax.ppermute(ahead, "gy", lay.cw)
        backward = lax.ppermute(behind, "gy", lay.ccw)
    return block(lay.place).astype(F32) + forward.astype(F32) + backward.astype(F32)


def partner(lay, axis, bit):
    size = lay.gx if axis == "gx" else lay.n
    return [(i, i ^ bit) for i in range(size)]


def spread(lay, own):
    across = lax.ppermute(own, "gx", partner(lay, "gx", 2))
    beside = lax.ppermute(own, "gx", partner(lay, "gx", 1))
    beyond = lax.ppermute(across, "gx", partner(lay, "gx", 1))
    return [own, across, beside, beyond]


def collect(lay, kept, sent):
    w = lay.width
    got = lax.ppermute(sent, "gx", partner(lay, "gx", 1))
    onward = (kept[:, w:].astype(F32) + got[:, w:].astype(F32)).astype(BF)
    across = lax.ppermute(onward, "gx", partner(lay, "gx", 2))
    return kept[:, :w].astype(F32) + got[:, :w].astype(F32) + across.astype(F32)


def halve(lay, value, axis, index):
    size = value.shape[0]
    while size > 1:
        bit = size // 2
        value = value.reshape((2, bit) + value.shape[1:])
        side = (index // bit) % 2
        sent = lax.dynamic_index_in_dim(value, 1 - side, 0, keepdims=False)
        kept = lax.dynamic_index_in_dim(value, side, 0, keepdims=False)
        value = kept + lax.ppermute(sent, axis, partner(lay, axis, bit))
        size = bit
    return value


def double(lay, value, axis, index):
    size, bit = (lay.gx if axis == "gx" else lay.n), 1
    value = value[None]
    while bit < size:
        other = lax.ppermute(value, axis, partner(lay, axis, bit))
        side = (index // bit) % 2
        low = jnp.where(side == 0, value, other)
        high = jnp.where(side == 0, other, value)
        value = jnp.concatenate([low, high], axis=0)
        bit *= 2
    return value


ACROSS = (((1,), (1,)), ((), ()))
DOWN = (((0,), (0,)), ((), ()))
PLAIN = (((1,), (0,)), ((), ()))
ROOT = 0.7978845608028654
CUBE = 0.044715
LO = IMG // 16 * 16
HI = (IMG + 15) // 16 * 16


def gelu(hidden):
    return 0.5 * hidden * (1.0 + jnp.tanh(ROOT * (hidden + CUBE * (hidden * hidden * hidden))))


def gelu_slope(hidden):
    square = hidden * hidden
    curve = jnp.tanh(ROOT * (hidden + CUBE * (square * hidden)))
    return 0.5 * (1.0 + curve) + 0.5 * hidden * (1.0 - curve * curve) * (
        ROOT * (1.0 + 3.0 * CUBE * square)
    )


def is_image_rows(count):
    return LO + lax.broadcasted_iota(jnp.int32, (HI - LO, count), 0) < IMG


def place_columns(sources, target, sems):
    copies, at = [], 0
    for k, source in enumerate(sources):
        size = source.shape[1]
        copies.append(pltpu.make_async_copy(source, target.at[:, at : at + size], sems.at[k]))
        at += size
    return copies


def store_rows(store, top, low):
    edge = jnp.where(is_image_rows(top.shape[1]), top[LO:HI], low[: HI - LO])
    store(slice(0, LO), top[:LO])
    store(slice(LO, HI), edge)
    store(slice(HI, None), low[HI - LO :])


ANY = pl.BlockSpec(memory_space=pl.ANY)


def forward_kernel(nx, narrays, nextra, runs, tile, finish, offsets, *refs):
    xs, arrays = refs[:nx], refs[nx : nx + narrays]
    extras = refs[nx + narrays : nx + narrays + nextra]
    outs = refs[nx + narrays + nextra : -4]
    xbuf, wbuf, xsem, wsem = refs[-4:]
    step, total = pl.program_id(0), pl.num_programs(0)
    slot = lax.rem(step, 2)

    def fetch(index, slot):
        columns = pl.ds(pl.multiple_of(index * tile, tile), tile)
        for k, (array, lead, row, count) in enumerate(runs):
            pltpu.make_async_copy(
                arrays[array].at[lead + (slice(None), slice(row, row + count), columns)],
                wbuf.at[slot, :, pl.ds(pl.multiple_of(offsets[k], 16), count), :],
                wsem.at[slot],
            ).start()

    @pl.when(step == 0)
    def _():
        for copy in place_columns(xs, xbuf, xsem):
            copy.start()
        fetch(0, 0)

    @pl.when(step + 1 < total)
    def _():
        fetch(step + 1, 1 - slot)

    @pl.when(step == 0)
    def _():
        for copy in place_columns(xs, xbuf, xsem):
            copy.wait()

    pltpu.make_async_copy(wbuf.at[slot], wbuf.at[slot], wsem.at[slot]).wait()
    top = jnp.dot(xbuf[:HI], wbuf[slot, 0], preferred_element_type=F32)
    low = jnp.dot(xbuf[LO:], wbuf[slot, 1], preferred_element_type=F32)
    store_rows(lambda where, value: finish(where, value, extras, outs), top, low)


def plain_finish(where, value, extras, outs):
    outs[0][where, :] = value.astype(outs[0].dtype)


def gelu_finish(where, value, extras, outs):
    outs[0][where, :] = value
    outs[1][where, :] = gelu(value).astype(BF)


def slope_finish(where, value, extras, outs):
    outs[0][where, :] = (gelu_slope(extras[0][where, :]) * value).astype(BF)


def forward_product(lay, xs, weight, tile, finish, out_types, extras=()):
    rows = xs[0].shape[0]
    depth = sum(x.shape[1] for x in xs)
    columns = weight.arrays[0].shape[-1]
    block = pl.BlockSpec((rows, tile), lambda i, _: (0, i))
    return pl.pallas_call(
        functools.partial(
            forward_kernel,
            len(xs),
            len(weight.arrays),
            len(extras),
            [run[:4] for run in weight.runs],
            tile,
            finish,
        ),
        grid_spec=pltpu.PrefetchScalarGridSpec(
            num_scalar_prefetch=1,
            grid=(columns // tile,),
            in_specs=[ANY] * (len(xs) + len(weight.arrays)) + [block] * len(extras),
            out_specs=[block] * len(out_types),
            scratch_shapes=[
                pltpu.VMEM((rows, depth), BF),
                pltpu.VMEM((2, 2, depth, tile), BF),
                pltpu.SemaphoreType.DMA((len(xs),)),
                pltpu.SemaphoreType.DMA((2,)),
            ],
        ),
        out_shape=[jax.ShapeDtypeStruct((rows, columns), dtype) for dtype in out_types],
        cost_estimate=pl.CostEstimate(
            flops=5 * rows * depth * columns,
            bytes_accessed=2 * (rows * depth + 2 * depth * columns + rows * columns),
            transcendentals=0,
        ),
    )(weight.offsets(lay), *xs, *weight.arrays, *extras)


def backward_kernel(nx, narrays, runs, tile, offsets, *refs):
    xs, arrays = refs[:nx], refs[nx : nx + narrays]
    kept, sent = refs[nx + narrays : nx + narrays + 2]
    xbuf, wbuf, xsem, wsem = refs[-4:]
    step, total = pl.program_id(0), pl.num_programs(0)
    half = total // 2
    slot = lax.rem(step, 2)

    def fetch(index, slot):
        first = lax.rem(index + half, total) * tile
        for k, (array, lead, row, count) in enumerate(runs):
            at = offsets[k] - first

            @pl.when(jnp.logical_and(at >= 0, at < tile))
            def _():
                pltpu.make_async_copy(
                    arrays[array].at[lead + (slice(None), slice(row, row + count))],
                    wbuf.at[slot, :, pl.ds(pl.multiple_of(at, 16), count), :],
                    wsem.at[slot],
                ).start()

    @pl.when(step == 0)
    def _():
        for copy in place_columns(xs, xbuf, xsem):
            copy.start()
        fetch(0, 0)

    @pl.when(step + 1 < total)
    def _():
        fetch(step + 1, 1 - slot)

    @pl.when(step == 0)
    def _():
        for copy in place_columns(xs, xbuf, xsem):
            copy.wait()

    pltpu.make_async_copy(wbuf.at[slot], wbuf.at[slot], wsem.at[slot]).wait()
    top = lax.dot_general(xbuf[:HI], wbuf[slot, 0], ACROSS, preferred_element_type=F32)
    low = lax.dot_general(xbuf[LO:], wbuf[slot, 1], ACROSS, preferred_element_type=F32)

    def write(out):
        def store(where, value):
            out[where, :] = value.astype(BF)

        store_rows(store, top, low)

    @pl.when(step < half)
    def _():
        write(sent)

    @pl.when(step >= half)
    def _():
        write(kept)


def backward_product(lay, xs, weight):
    rows = xs[0].shape[0]
    depth = sum(x.shape[1] for x in xs)
    tile = lay.width
    columns = tile * lay.gx
    total = lay.gx
    half = total // 2
    return pl.pallas_call(
        functools.partial(
            backward_kernel,
            len(xs),
            len(weight.arrays),
            [run[:4] for run in weight.runs],
            tile,
        ),
        grid_spec=pltpu.PrefetchScalarGridSpec(
            num_scalar_prefetch=1,
            grid=(total,),
            in_specs=[ANY] * (len(xs) + len(weight.arrays)),
            out_specs=[
                pl.BlockSpec((rows, tile), lambda i, _: (0, jnp.maximum(i - half, 0))),
                pl.BlockSpec((rows, tile), lambda i, _: (0, jnp.minimum(i, half - 1))),
            ],
            scratch_shapes=[
                pltpu.VMEM((rows, depth), BF),
                pltpu.VMEM((2, 2, tile, depth), BF),
                pltpu.SemaphoreType.DMA((len(xs),)),
                pltpu.SemaphoreType.DMA((2,)),
            ],
        ),
        out_shape=[jax.ShapeDtypeStruct((rows, columns // 2), BF)] * 2,
        cost_estimate=pl.CostEstimate(
            flops=5 * rows * depth * columns,
            bytes_accessed=2 * (rows * depth + 2 * depth * columns + rows * columns),
            transcendentals=0,
        ),
    )(weight.offsets(lay), *xs, *weight.arrays)


def weight_kernel(nleft, nright, blocks, *refs):
    lefts, rights = refs[:nleft], refs[nleft : nleft + nright]
    out = refs[nleft + nright]
    lbuf, rbuf, lsem, rsem = refs[-4:]
    step = pl.program_id(0)

    def left_copies():
        return [
            pltpu.make_async_copy(left, lbuf.at[k], lsem.at[k]) for k, left in enumerate(lefts)
        ]

    @pl.when(step == 0)
    def _():
        for copy in place_columns(rights, rbuf, rsem) + left_copies():
            copy.start()
        for copy in place_columns(rights, rbuf, rsem) + left_copies():
            copy.wait()

    block = lbuf[step]
    edge = block[LO:HI]
    image = is_image_rows(edge.shape[1])
    zero = jnp.zeros_like(edge)
    top = jnp.concatenate([block[:LO], jnp.where(image, edge, zero)], axis=0)
    low = jnp.concatenate([jnp.where(image, zero, edge), block[HI:]], axis=0)
    top = lax.dot_general(top, rbuf[:HI], DOWN, preferred_element_type=F32).astype(BF)
    low = lax.dot_general(low, rbuf[LO:], DOWN, preferred_element_type=F32).astype(BF)
    count = out.shape[2]
    for k in range(out.shape[0]):
        out[k, 0] = top[k * count : (k + 1) * count]
        out[k, 1] = low[k * count : (k + 1) * count]


def weight_product(lay, lefts, rights):
    rows, width = lefts[0].shape
    depth = width * len(lefts)
    columns = sum(right.shape[1] for right in rights)
    per = lay.width // lay.rows
    blocks = jnp.stack([lay.mx, lay.mx ^ 2, lay.mx ^ 1, lay.mx ^ 3]).astype(jnp.int32)
    return pl.pallas_call(
        functools.partial(weight_kernel, len(lefts), len(rights)),
        grid_spec=pltpu.PrefetchScalarGridSpec(
            num_scalar_prefetch=1,
            grid=(len(lefts),),
            in_specs=[ANY] * (len(lefts) + len(rights)),
            out_specs=pl.BlockSpec(
                (per, 2, lay.rows, columns), lambda i, blocks: (blocks[i], 0, 0, 0)
            ),
            scratch_shapes=[
                pltpu.VMEM((len(lefts), rows, width), BF),
                pltpu.VMEM((rows, columns), BF),
                pltpu.SemaphoreType.DMA((len(lefts),)),
                pltpu.SemaphoreType.DMA((len(rights),)),
            ],
        ),
        out_shape=jax.ShapeDtypeStruct((lay.n, 2, lay.rows, columns), BF),
        cost_estimate=pl.CostEstimate(
            flops=5 * rows * depth * columns,
            bytes_accessed=2 * (rows * depth + 2 * depth * columns + rows * columns),
            transcendentals=0,
        ),
    )(blocks, *lefts, *rights)


def only_head(block, head):
    lane = lax.broadcasted_iota(jnp.int32, block.shape, 1)
    return jnp.where(lane // HD == head, block, jnp.zeros_like(block))


def attend_kernel(q_ref, k_ref, v_ref, mix_ref, log_ref, turned):
    @pl.when(pl.program_id(1) == 0)
    def _():
        turned[...] = v_ref[...].T

    halves = []
    for head in range(2):
        query = only_head(q_ref[...], head)
        scores = lax.dot_general(k_ref[...], query, ACROSS, preferred_element_type=F32) * 0.125
        highest = jnp.max(scores, axis=0, keepdims=True)
        powers = jnp.exp(scores - highest)
        total = jnp.sum(powers, axis=0, keepdims=True)
        shares = (powers * (1.0 / total)).astype(BF)
        values = turned[head * HD : (head + 1) * HD, :]
        halves.append(lax.dot_general(values, shares, PLAIN, preferred_element_type=F32))
        log_ref[0, head : head + 1, :] = highest + jnp.log(total)
    mix_ref[...] = jnp.concatenate(halves, axis=0).T.astype(BF)


def attention(projected, pair, chunk):
    rows, columns = projected.shape
    width = columns // 3
    pairs = width // (2 * HD)
    lanes = 2 * HD
    return pl.pallas_call(
        attend_kernel,
        grid=(1, rows // chunk),
        in_specs=[
            pl.BlockSpec((chunk, lanes), lambda p, i: (i, pair)),
            pl.BlockSpec((rows, lanes), lambda p, i: (0, pairs + pair)),
            pl.BlockSpec((rows, lanes), lambda p, i: (0, 2 * pairs + pair)),
        ],
        out_specs=[
            pl.BlockSpec((chunk, lanes), lambda p, i: (i, 0)),
            pl.BlockSpec((1, 2, chunk), lambda p, i: (0, 0, i)),
        ],
        scratch_shapes=[pltpu.VMEM((lanes, rows), BF)],
        out_shape=[
            jax.ShapeDtypeStruct((rows, lanes), BF),
            jax.ShapeDtypeStruct((1, 2, rows), F32),
        ],
        cost_estimate=pl.CostEstimate(
            flops=72 * rows * rows * lanes, bytes_accessed=8 * rows * lanes, transcendentals=0
        ),
    )(projected, projected, projected)


def attend_back_kernel(
    q_ref, k_ref, v_ref, log_ref, up_ref, dq_ref, dk_ref, dv_ref, turned, key_sum, value_sum
):
    step = pl.program_id(1)

    @pl.when(step == 0)
    def _():
        turned[...] = k_ref[...].T
        key_sum[...] = jnp.zeros_like(key_sum)
        value_sum[...] = jnp.zeros_like(value_sum)

    halves = []
    for head in range(2):
        query = only_head(q_ref[...], head)
        upstream = only_head(up_ref[...], head)
        scores = lax.dot_general(k_ref[...], query, ACROSS, preferred_element_type=F32) * 0.125
        shares = jnp.exp(scores - log_ref[0, head : head + 1, :])
        value_sum[...] += lax.dot_general(
            shares.astype(BF), upstream, PLAIN, preferred_element_type=F32
        )
        slope = lax.dot_general(v_ref[...], upstream, ACROSS, preferred_element_type=F32)
        inner = jnp.sum(shares * slope, axis=0, keepdims=True)
        score_grad = (shares * (slope - inner)).astype(BF)
        key_sum[...] += lax.dot_general(score_grad, query, PLAIN, preferred_element_type=F32)
        keys = turned[head * HD : (head + 1) * HD, :]
        halves.append(lax.dot_general(keys, score_grad, PLAIN, preferred_element_type=F32))
    dq_ref[...] = (jnp.concatenate(halves, axis=0).T * 0.125).astype(BF)

    @pl.when(step == pl.num_programs(1) - 1)
    def _():
        dk_ref[...] = (key_sum[...] * 0.125).astype(BF)
        dv_ref[...] = value_sum[...].astype(BF)


def attention_back(projected, logsum, upstream, pair, chunk):
    rows, columns = projected.shape
    width = columns // 3
    pairs = width // (2 * HD)
    lanes = 2 * HD
    part = pl.BlockSpec((chunk, lanes), lambda p, i: (i, 0))
    whole = pl.BlockSpec((rows, lanes), lambda p, i: (0, 0))
    return pl.pallas_call(
        attend_back_kernel,
        grid=(1, rows // chunk),
        in_specs=[
            pl.BlockSpec((chunk, lanes), lambda p, i: (i, pair)),
            pl.BlockSpec((rows, lanes), lambda p, i: (0, pairs + pair)),
            pl.BlockSpec((rows, lanes), lambda p, i: (0, 2 * pairs + pair)),
            pl.BlockSpec((1, 2, chunk), lambda p, i: (0, 0, i)),
            pl.BlockSpec((chunk, lanes), lambda p, i: (i, pair)),
        ],
        out_specs=[part, whole, whole],
        scratch_shapes=[
            pltpu.VMEM((lanes, rows), BF),
            pltpu.VMEM((rows, lanes), F32),
            pltpu.VMEM((rows, lanes), F32),
        ],
        out_shape=[jax.ShapeDtypeStruct((rows, lanes), BF)] * 3,
        cost_estimate=pl.CostEstimate(
            flops=90 * rows * rows * lanes, bytes_accessed=16 * rows * lanes, transcendentals=0
        ),
    )(projected, projected, projected, logsum, upstream)


def after(value, *others):
    return lax.optimization_barrier((value,) + others)[0]


def on_device(
    image,
    text,
    condition,
    attend_weight,
    output_weight,
    up_weight,
    down_weight,
    adaptive_weight,
    image_cotangent,
    text_cotangent,
):
    width = image.shape[1]
    rows = IMG + TXT
    lay = Layout(width)
    full_width = width * lay.gx
    is_image = (jnp.arange(rows) < IMG)[:, None]

    def per_row(pair):
        return jnp.where(is_image, pair[0][None, :], pair[1][None, :])

    def row_sums(value):
        top = jnp.sum(jnp.where(is_image, value, 0.0), axis=0)
        low = jnp.sum(jnp.where(is_image, 0.0, value), axis=0)
        return jnp.stack([top, low])

    activated = jax.nn.silu(condition.astype(F32)).astype(BF)
    partial_mod = jnp.einsum(
        "sd,qdcx->sqcx", activated, adaptive_weight[0], preferred_element_type=F32
    )
    factors = halve(lay, partial_mod, "gy", lay.me)[0]
    attend_shard = attend_weight[0].reshape(2, lay.rows, 3 * width)
    output_shard = jnp.swapaxes(output_weight[0], 1, 2)
    down_shard = jnp.swapaxes(down_weight[0], 1, 2)
    attend_full = ring_gather(lay, after(attend_shard, factors))
    output_full = ring_gather(lay, after(output_shard, attend_full.arrays[5]))
    up_full = ring_gather(lay, after(up_weight[0], attend_full.arrays[5]))
    down_full = ring_gather(lay, after(down_shard, output_full.arrays[5]))

    shift1, scale1, gate1, shift2, scale2, gate2 = [
        per_row(factors[:, k]) for k in range(6)
    ]

    def totals_of(first, second):
        totals = lax.psum(jnp.stack([jnp.sum(first, axis=1), jnp.sum(second, axis=1)]), "gx")
        return totals[0][:, None] / full_width, totals[1][:, None] / full_width

    def normalize(value, shift, scale):
        average, square = totals_of(value, value * value)
        inverse = lax.rsqrt(square - average * average + EPSILON)
        unit = (value - average) * inverse
        lowered = (unit * (1.0 + scale) + shift).astype(BF)
        return unit, inverse, spread(lay, lowered)

    def norm_back(grad, unit, inverse, scale):
        scaled = grad * (1.0 + scale)
        mean, inner = totals_of(scaled, scaled * unit)
        result = inverse * (scaled - mean - unit * inner)
        return result, row_sums(grad * unit), row_sums(grad)

    stream = jnp.concatenate([image, text], axis=0).astype(F32)
    cotangent = jnp.concatenate([image_cotangent, text_cotangent], axis=0).astype(F32)

    unit1, inverse1, first_full = normalize(stream, shift1, scale1)
    feed_full = spread(lay, (gate2 * cotangent).astype(BF))

    def forward(*rest):
        return forward_product(lay, *rest)

    def backward(*rest):
        return backward_product(lay, *rest)

    def product(*rest):
        return weight_product(lay, *rest)

    pairs = width // (2 * HD)
    projected = forward(first_full, attend_full, width, plain_finish, [BF])[0]
    mixtures, logsums = [], []
    for pair in range(pairs):
        source = after(projected, mixtures[-1]) if mixtures else projected
        mixture, logsum = attention(source, pair, 256)
        mixtures.append(mixture)
        logsums.append(logsum)
    branch = collect(lay, *backward(mixtures, output_full))
    middle = stream + gate1 * branch
    unit2, inverse2, second_full = normalize(middle, shift2, scale2)
    hidden, active = forward(second_full, up_full, 512, gelu_finish, [F32, BF])
    down_grad = ring_scatter(lay, product(feed_full, [active]))

    hidden_grad = forward(feed_full, down_full, 512, slope_finish, [BF], [hidden])[0]
    second_partial = backward([hidden_grad], up_full)
    second_grad = collect(lay, *second_partial)
    up_local = product(second_full, [after(hidden_grad, second_partial[1])])
    up_grad = ring_scatter(lay, up_local)
    feed = collect(lay, *backward([after(active, up_local)], down_full))
    result = middle + gate2 * feed
    gate2_grad = row_sums(cotangent * feed)
    middle_part, scale2_grad, shift2_grad = norm_back(second_grad, unit2, inverse2, scale2)
    middle_grad = cotangent + middle_part
    gate1_grad = row_sums(middle_grad * branch)
    branch_full = spread(lay, (gate1 * middle_grad).astype(BF))
    mixed_grad = forward(branch_full, output_full, width, plain_finish, [BF])[0]
    output_local = product(branch_full, mixtures)
    output_grad = ring_scatter(lay, output_local)
    parts = []
    for pair in range(pairs):
        source = after(mixed_grad, parts[-1][0]) if parts else mixed_grad
        parts.append(attention_back(projected, logsums[pair], source, pair, 256))
    projected_grad = [parts[pair][k] for k in range(3) for pair in range(pairs)]
    attend_local = product(first_full, projected_grad)
    attend_grad = ring_scatter(lay, attend_local)
    first_grad = collect(lay, *backward(projected_grad, attend_full))
    input_part, scale1_grad, shift1_grad = norm_back(first_grad, unit1, inverse1, scale1)
    input_grad = middle_grad + input_part

    modulation_grad = jnp.stack(
        [shift1_grad, scale1_grad, gate1_grad, shift2_grad, scale2_grad, gate2_grad], axis=1
    ).astype(BF)
    all_mod = double(lay, modulation_grad, "gy", lay.me)
    adaptive_grad = jnp.einsum("sd,sqcx->qdcx", activated, all_mod, preferred_element_type=F32)
    condition_partial = jnp.einsum(
        "sqcx,qdcx->sd", all_mod, adaptive_weight[0], preferred_element_type=F32
    )
    share_rows = condition.shape[0] // lay.gx
    condition_share = halve(
        lay, condition_partial.reshape(lay.gx, share_rows, -1), "gx", lay.mx
    )[0]
    own_condition = lax.dynamic_slice_in_dim(condition, lay.mx * share_rows, share_rows, 0)
    _, silu_pullback = jax.vjp(jax.nn.silu, own_condition.astype(F32))
    condition_grad = silu_pullback(condition_share)[0]
    return (
        result[:IMG].astype(BF),
        result[IMG:].astype(BF),
        input_grad[:IMG],
        input_grad[IMG:],
        condition_grad,
        attend_grad.reshape((1,) + attend_weight.shape[1:]),
        jnp.swapaxes(output_grad, 1, 2)[None],
        up_grad[None],
        jnp.swapaxes(down_grad, 1, 2)[None],
        adaptive_grad[None],
    )


def solution(mesh):
    placed = (
        P("gy", "gx"),
        P("gy", "gx"),
        P(None, "gy"),
        P(None, None, "gy", None, "gx"),
        P(None, None, "gx", "gy"),
        P(None, None, "gy", "gx"),
        P(None, None, "gx", "gy"),
        P(None, None, "gy", None, "gx"),
        P("gy", "gx"),
        P("gy", "gx"),
    )

    return jax.shard_map(
        on_device,
        mesh=mesh,
        in_specs=placed,
        out_specs=(
            P("gy", "gx"),
            P("gy", "gx"),
            P("gy", "gx"),
            P("gy", "gx"),
            P("gx", "gy"),
            P(None, None, "gy", None, "gx"),
            P(None, None, "gx", "gy"),
            P(None, None, "gy", "gx"),
            P(None, None, "gx", "gy"),
            P(None, None, "gy", None, "gx"),
        ),
        check_vma=False,
    )
```

```python
import functools

import jax
import jax.numpy as jnp
from jax import lax
from jax.experimental import pallas as pl
from jax.experimental.pallas import tpu as pltpu
from jax.sharding import PartitionSpec as P


HD = 64
IMG = 870
TXT = 154
EPSILON = 1e-06


BF = jnp.bfloat16
F32 = jnp.float32


def ring_order(n):
    return [2 * p if p < n // 2 else 2 * (n - 1 - p) + 1 for p in range(n)]


def ring_place(index, n):
    return jnp.where(index % 2 == 0, index // 2, n - 1 - index // 2)


def ring_member(place, n):
    place = place % n
    return jnp.where(place < n // 2, 2 * place, 2 * (n - 1 - place) + 1)


class Layout:
    def __init__(self, width):
        self.n = lax.axis_size("gy")
        self.gx = lax.axis_size("gx")
        self.me = lax.axis_index("gy")
        self.mx = lax.axis_index("gx")
        self.place = ring_place(self.me, self.n)
        self.width = width
        self.rows = width * self.gx // self.n
        order = ring_order(self.n)
        self.cw = [(order[i], order[(i + 1) % self.n]) for i in range(self.n)]
        self.ccw = [(b, a) for a, b in self.cw]

    def offset(self, owner):
        per = self.width // self.rows
        relative = (owner // per) ^ self.mx
        swapped = (relative % 2) * 2 + relative // 2
        return swapped * self.width + (owner % per) * self.rows


class Gathered:
    def __init__(self, arrays, runs):
        self.arrays, self.runs = arrays, runs

    def offsets(self, lay):
        return jnp.stack(
            [lay.offset(owner) + inner for _, _, _, _, owner, inner in self.runs]
        ).astype(jnp.int32)


def first_half(rows):
    return (rows // 2 + 15) // 16 * 16


def ring_gather(lay, shard):
    rows, far = lay.rows, lay.n // 2
    half = first_half(rows)
    arrays, runs = [shard], [(0, (), 0, rows, lay.me, 0)]
    forward = backward = shard
    for k in range(1, far):
        forward = lax.ppermute(forward, "gy", lay.cw)
        backward = lax.ppermute(backward, "gy", lay.ccw)
        runs.append((len(arrays), (), 0, rows, ring_member(lay.place - k + lay.n, lay.n), 0))
        runs.append((len(arrays) + 1, (), 0, rows, ring_member(lay.place + k, lay.n), 0))
        arrays += [forward, backward]
    last = ring_member(lay.place + far, lay.n)
    runs.append((len(arrays), (), 0, half, last, 0))
    runs.append((len(arrays) + 1, (), 0, rows - half, last, half))
    arrays.append(lax.ppermute(forward[:, :half], "gy", lay.cw))
    arrays.append(lax.ppermute(backward[:, half:], "gy", lay.ccw))
    return Gathered(arrays, runs)


def ring_scatter(lay, local, parts=1):
    full, forward, backward = local
    far = lay.n // 2

    def send(forward, backward):
        forward = lax.ppermute(forward, "gy", lay.cw)
        backward = lax.ppermute(backward, "gy", lay.ccw)
        return forward, backward

    forward, backward = send(forward, backward)
    for k in range(far - 1, 0, -1):
        ahead = ring_member(lay.place + k + lay.n, lay.n)
        behind = ring_member(lay.place - k + lay.n, lay.n)
        forward, backward = ring_add(forward, backward, full, ahead, behind)
        forward, backward = send(forward, backward)
    own = lax.dynamic_index_in_dim(full, lay.me, 0, keepdims=False)
    if parts == 1:
        return own.astype(F32) + forward.astype(F32) + backward.astype(F32)
    pieces = zip(*[jnp.split(value, parts, axis=2) for value in (own, forward, backward)])
    return jnp.stack([a.astype(F32) + b.astype(F32) + c.astype(F32) for a, b, c in pieces], axis=2)


def partner(lay, axis, bit):
    size = lay.gx if axis == "gx" else lay.n
    return [(i, i ^ bit) for i in range(size)]


def spread(lay, own):
    across = lax.ppermute(own, "gx", partner(lay, "gx", 2))
    beside = lax.ppermute(own, "gx", partner(lay, "gx", 1))
    beyond = lax.ppermute(across, "gx", partner(lay, "gx", 1))
    return [own, across, beside, beyond]


def collect(lay, kept, sent, late=None):
    w = lay.width
    got = lax.ppermute(sent, "gx", partner(lay, "gx", 1))
    onward = (kept[:, w:].astype(F32) + got[:, w:].astype(F32)).astype(BF)
    across = lax.ppermute(onward, "gx", partner(lay, "gx", 2))
    if late is not None:
        kept, got, across, _ = lax.optimization_barrier((kept, got, across, late))
    return kept[:, :w].astype(F32) + got[:, :w].astype(F32) + across.astype(F32)


def halve(lay, value, axis, index):
    size = value.shape[0]
    while size > 1:
        bit = size // 2
        value = value.reshape((2, bit) + value.shape[1:])
        side = (index // bit) % 2
        sent = lax.dynamic_index_in_dim(value, 1 - side, 0, keepdims=False)
        kept = lax.dynamic_index_in_dim(value, side, 0, keepdims=False)
        value = kept + lax.ppermute(sent, axis, partner(lay, axis, bit))
        size = bit
    return value


def double(lay, value, axis, index):
    size, bit = (lay.gx if axis == "gx" else lay.n), 1
    value = value[None]
    while bit < size:
        other = lax.ppermute(value, axis, partner(lay, axis, bit))
        side = (index // bit) % 2
        low = jnp.where(side == 0, value, other)
        high = jnp.where(side == 0, other, value)
        value = jnp.concatenate([low, high], axis=0)
        bit *= 2
    return value


ACROSS = (((1,), (1,)), ((), ()))
DOWN = (((0,), (0,)), ((), ()))
PLAIN = (((1,), (0,)), ((), ()))
ROOT = 0.7978845608028654
CUBE = 0.044715
LO = IMG // 16 * 16
HI = (IMG + 15) // 16 * 16


def gelu(hidden):
    return 0.5 * hidden * (1.0 + jnp.tanh(ROOT * (hidden + CUBE * (hidden * hidden * hidden))))


def gelu_slope(hidden):
    square = hidden * hidden
    curve = jnp.tanh(ROOT * (hidden + CUBE * (square * hidden)))
    return 0.5 * (1.0 + curve) + 0.5 * hidden * (1.0 - curve * curve) * (
        ROOT * (1.0 + 3.0 * CUBE * square)
    )


def is_image_rows(count):
    return LO + lax.broadcasted_iota(jnp.int32, (HI - LO, count), 0) < IMG


def place_columns(sources, target, sems):
    copies, at = [], 0
    for k, source in enumerate(sources):
        size = source.shape[1]
        copies.append(pltpu.make_async_copy(source, target.at[:, at : at + size], sems.at[k]))
        at += size
    return copies


def store_rows(store, top, low):
    edge = jnp.where(is_image_rows(top.shape[1]), top[LO:HI], low[: HI - LO])
    store(slice(0, LO), top[:LO])
    store(slice(LO, HI), edge)
    store(slice(HI, None), low[HI - LO :])


ANY = pl.BlockSpec(memory_space=pl.ANY)


def forward_kernel(nx, narrays, nextra, runs, tile, finish, offsets, *refs):
    xs, arrays = refs[:nx], refs[nx : nx + narrays]
    extras = refs[nx + narrays : nx + narrays + nextra]
    outs = refs[nx + narrays + nextra : -4]
    xbuf, wbuf, xsem, wsem = refs[-4:]
    step, total = pl.program_id(0), pl.num_programs(0)
    slot = lax.rem(step, 2)

    def fetch(index, slot):
        columns = pl.ds(pl.multiple_of(index * tile, tile), tile)
        for k, (array, lead, row, count) in enumerate(runs):
            pltpu.make_async_copy(
                arrays[array].at[lead + (slice(None), slice(row, row + count), columns)],
                wbuf.at[slot, :, pl.ds(pl.multiple_of(offsets[k], 16), count), :],
                wsem.at[slot],
            ).start()

    @pl.when(step == 0)
    def _():
        for copy in place_columns(xs, xbuf, xsem):
            copy.start()
        fetch(0, 0)

    @pl.when(step + 1 < total)
    def _():
        fetch(step + 1, 1 - slot)

    @pl.when(step == 0)
    def _():
        for copy in place_columns(xs, xbuf, xsem):
            copy.wait()

    pltpu.make_async_copy(wbuf.at[slot], wbuf.at[slot], wsem.at[slot]).wait()
    top = jnp.dot(xbuf[:HI], wbuf[slot, 0], preferred_element_type=F32)
    low = jnp.dot(xbuf[LO:], wbuf[slot, 1], preferred_element_type=F32)
    store_rows(lambda where, value: finish(where, value, extras, outs), top, low)


def plain_finish(where, value, extras, outs):
    outs[0][where, :] = value.astype(outs[0].dtype)


def gelu_finish(where, value, extras, outs):
    outs[0][where, :] = value
    outs[1][where, :] = gelu(value).astype(BF)


def slope_finish(where, value, extras, outs):
    outs[0][where, :] = (gelu_slope(extras[0][where, :]) * value).astype(BF)


def forward_product(lay, xs, weight, tile, finish, out_types, extras=()):
    rows = xs[0].shape[0]
    depth = sum(x.shape[1] for x in xs)
    columns = weight.arrays[0].shape[-1]
    block = pl.BlockSpec((rows, tile), lambda i, _: (0, i))
    return pl.pallas_call(
        functools.partial(
            forward_kernel,
            len(xs),
            len(weight.arrays),
            len(extras),
            [run[:4] for run in weight.runs],
            tile,
            finish,
        ),
        grid_spec=pltpu.PrefetchScalarGridSpec(
            num_scalar_prefetch=1,
            grid=(columns // tile,),
            in_specs=[ANY] * (len(xs) + len(weight.arrays)) + [block] * len(extras),
            out_specs=[block] * len(out_types),
            scratch_shapes=[
                pltpu.VMEM((rows, depth), BF),
                pltpu.VMEM((2, 2, depth, tile), BF),
                pltpu.SemaphoreType.DMA((len(xs),)),
                pltpu.SemaphoreType.DMA((2,)),
            ],
        ),
        out_shape=[jax.ShapeDtypeStruct((rows, columns), dtype) for dtype in out_types],
        cost_estimate=pl.CostEstimate(
            flops=5 * rows * depth * columns,
            bytes_accessed=2 * (rows * depth + 2 * depth * columns + rows * columns),
            transcendentals=0,
        ),
    )(weight.offsets(lay), *xs, *weight.arrays, *extras)


def backward_kernel(nx, narrays, runs, tile, offsets, *refs):
    xs, arrays = refs[:nx], refs[nx : nx + narrays]
    kept, sent = refs[nx + narrays : nx + narrays + 2]
    xbuf, wbuf, xsem, wsem = refs[-4:]
    step, total = pl.program_id(0), pl.num_programs(0)
    half = total // 2
    slot = lax.rem(step, 2)

    def fetch(index, slot):
        first = lax.rem(index + half, total) * tile
        for k, (array, lead, row, count) in enumerate(runs):
            at = offsets[k] - first

            @pl.when(jnp.logical_and(at >= 0, at < tile))
            def _():
                pltpu.make_async_copy(
                    arrays[array].at[lead + (slice(None), slice(row, row + count))],
                    wbuf.at[slot, :, pl.ds(pl.multiple_of(at, 16), count), :],
                    wsem.at[slot],
                ).start()

    @pl.when(step == 0)
    def _():
        for copy in place_columns(xs, xbuf, xsem):
            copy.start()
        fetch(0, 0)

    @pl.when(step + 1 < total)
    def _():
        fetch(step + 1, 1 - slot)

    @pl.when(step == 0)
    def _():
        for copy in place_columns(xs, xbuf, xsem):
            copy.wait()

    pltpu.make_async_copy(wbuf.at[slot], wbuf.at[slot], wsem.at[slot]).wait()
    top = lax.dot_general(xbuf[:HI], wbuf[slot, 0], ACROSS, preferred_element_type=F32)
    low = lax.dot_general(xbuf[LO:], wbuf[slot, 1], ACROSS, preferred_element_type=F32)

    def write(out):
        def store(where, value):
            out[where, :] = value.astype(BF)

        store_rows(store, top, low)

    @pl.when(step < half)
    def _():
        write(sent)

    @pl.when(step >= half)
    def _():
        write(kept)


def backward_product(lay, xs, weight):
    rows = xs[0].shape[0]
    depth = sum(x.shape[1] for x in xs)
    tile = lay.width
    columns = tile * lay.gx
    total = lay.gx
    half = total // 2
    return pl.pallas_call(
        functools.partial(
            backward_kernel,
            len(xs),
            len(weight.arrays),
            [run[:4] for run in weight.runs],
            tile,
        ),
        grid_spec=pltpu.PrefetchScalarGridSpec(
            num_scalar_prefetch=1,
            grid=(total,),
            in_specs=[ANY] * (len(xs) + len(weight.arrays)),
            out_specs=[
                pl.BlockSpec((rows, tile), lambda i, _: (0, jnp.maximum(i - half, 0))),
                pl.BlockSpec((rows, tile), lambda i, _: (0, jnp.minimum(i, half - 1))),
            ],
            scratch_shapes=[
                pltpu.VMEM((rows, depth), BF),
                pltpu.VMEM((2, 2, tile, depth), BF),
                pltpu.SemaphoreType.DMA((len(xs),)),
                pltpu.SemaphoreType.DMA((2,)),
            ],
        ),
        out_shape=[jax.ShapeDtypeStruct((rows, columns // 2), BF)] * 2,
        cost_estimate=pl.CostEstimate(
            flops=5 * rows * depth * columns,
            bytes_accessed=2 * (rows * depth + 2 * depth * columns + rows * columns),
            transcendentals=0,
        ),
    )(weight.offsets(lay), *xs, *weight.arrays)


def weight_kernel(nleft, nright, blocks, *refs):
    lefts, rights = refs[:nleft], refs[nleft : nleft + nright]
    out, ahead, behind, lbuf, rbuf, tbuf, lsem, rsem = refs[nleft + nright :]
    step = pl.program_id(0)

    def left_copies():
        return [
            pltpu.make_async_copy(left, lbuf.at[k], lsem.at[k]) for k, left in enumerate(lefts)
        ]

    @pl.when(step == 0)
    def _():
        first, *others = left_copies()
        for copy in [first] + place_columns(rights, rbuf, rsem) + others:
            copy.start()
        for copy in place_columns(rights, rbuf, rsem):
            copy.wait()
        edge = rbuf[LO:HI]
        image = is_image_rows(edge.shape[1])
        zero = jnp.zeros_like(edge)
        tbuf[: HI - LO] = jnp.where(image, zero, edge)
        tbuf[HI - LO :] = rbuf[HI:]
        rbuf[LO:HI] = jnp.where(image, edge, zero)

    pltpu.make_async_copy(lbuf.at[step], lbuf.at[step], lsem.at[step]).wait()
    top = lax.dot_general(lbuf[step, :HI], rbuf[:HI], DOWN, preferred_element_type=F32)
    low = lax.dot_general(lbuf[step, LO:], tbuf[...], DOWN, preferred_element_type=F32)
    top, low = top.astype(BF), low.astype(BF)
    per, _, count, _ = out.shape
    for k in range(per):
        rows = slice(k * count, (k + 1) * count)
        out[k, 0] = top[rows]
        out[k, 1] = low[rows]

        @pl.when(blocks[step] * per + k == blocks[nleft])
        def _():
            half = ahead.shape[1]
            ahead[0] = top[rows][:half]
            ahead[1] = low[rows][:half]
            behind[0] = top[rows][half:]
            behind[1] = low[rows][half:]


def weight_product(lay, lefts, rights):
    rows, width = lefts[0].shape
    depth = width * len(lefts)
    columns = sum(right.shape[1] for right in rights)
    per = lay.width // lay.rows
    half = first_half(lay.rows)
    last = ring_member(lay.place + lay.n // 2, lay.n)
    blocks = jnp.stack([lay.mx, lay.mx ^ 2, lay.mx ^ 1, lay.mx ^ 3, last]).astype(jnp.int32)
    return pl.pallas_call(
        functools.partial(weight_kernel, len(lefts), len(rights)),
        grid_spec=pltpu.PrefetchScalarGridSpec(
            num_scalar_prefetch=1,
            grid=(len(lefts),),
            in_specs=[ANY] * (len(lefts) + len(rights)),
            out_specs=[
                pl.BlockSpec((per, 2, lay.rows, columns), lambda i, blocks: (blocks[i], 0, 0, 0)),
                pl.BlockSpec((2, half, columns), lambda i, blocks: (0, 0, 0)),
                pl.BlockSpec((2, lay.rows - half, columns), lambda i, blocks: (0, 0, 0)),
            ],
            scratch_shapes=[
                pltpu.VMEM((len(lefts), rows, width), BF),
                pltpu.VMEM((rows, columns), BF),
                pltpu.VMEM((rows - LO, columns), BF),
                pltpu.SemaphoreType.DMA((len(lefts),)),
                pltpu.SemaphoreType.DMA((len(rights),)),
            ],
        ),
        out_shape=[
            jax.ShapeDtypeStruct((lay.n, 2, lay.rows, columns), BF),
            jax.ShapeDtypeStruct((2, half, columns), BF),
            jax.ShapeDtypeStruct((2, lay.rows - half, columns), BF),
        ],
        cost_estimate=pl.CostEstimate(
            flops=5 * rows * depth * columns,
            bytes_accessed=2 * (rows * depth + 2 * depth * columns + rows * columns),
            transcendentals=0,
        ),
    )(blocks, *lefts, *rights)


def add_kernel(owners, forward, backward, ahead, behind, forward_out, backward_out):
    half, other = forward.shape[1], backward.shape[1]
    rows = ahead.shape[2]
    forward_out[0, :half] = forward[0] + ahead[0, 0, :half]
    backward_out[0, rows - other :] = backward[0] + behind[0, 0, rows - other :]
    if half < rows:
        forward_out[0, half:] = ahead[0, 0, half:]
        backward_out[0, : rows - other] = behind[0, 0, : rows - other]


def ring_add(forward, backward, full, ahead, behind):
    _, _, rows, columns = full.shape
    owners = jnp.stack([ahead, behind]).astype(jnp.int32)

    def moving(value):
        return pl.BlockSpec((1, value.shape[1], columns), lambda s, _: (s, 0, 0))

    out = pl.BlockSpec((1, rows, columns), lambda s, _: (s, 0, 0))
    return pl.pallas_call(
        add_kernel,
        grid_spec=pltpu.PrefetchScalarGridSpec(
            num_scalar_prefetch=1,
            grid=(2,),
            in_specs=[
                moving(forward),
                moving(backward),
                pl.BlockSpec((1, 1, rows, columns), lambda s, owners: (owners[0], s, 0, 0)),
                pl.BlockSpec((1, 1, rows, columns), lambda s, owners: (owners[1], s, 0, 0)),
            ],
            out_specs=[out, out],
        ),
        out_shape=[jax.ShapeDtypeStruct((2, rows, columns), BF)] * 2,
        cost_estimate=pl.CostEstimate(
            flops=10000 * rows * columns, bytes_accessed=24 * rows * columns, transcendentals=0
        ),
    )(owners, forward, backward, full, full)


def only_head(block, head):
    lane = lax.broadcasted_iota(jnp.int32, block.shape, 1)
    return jnp.where(lane // HD == head, block, jnp.zeros_like(block))


def attend_kernel(q_ref, k_ref, v_ref, mix_ref, log_ref, turned):
    @pl.when(pl.program_id(1) == 0)
    def _():
        turned[...] = v_ref[...].T

    halves = []
    for head in range(2):
        query = only_head(q_ref[...], head)
        scores = lax.dot_general(k_ref[...], query, ACROSS, preferred_element_type=F32) * 0.125
        highest = jnp.max(scores, axis=0, keepdims=True)
        powers = jnp.exp(scores - highest)
        total = jnp.sum(powers, axis=0, keepdims=True)
        shares = (powers * (1.0 / total)).astype(BF)
        values = turned[head * HD : (head + 1) * HD, :]
        halves.append(lax.dot_general(values, shares, PLAIN, preferred_element_type=F32))
        log_ref[0, head : head + 1, :] = highest + jnp.log(total)
    mix_ref[...] = jnp.concatenate(halves, axis=0).T.astype(BF)


def attention(projected, pair, chunk):
    rows, columns = projected.shape
    width = columns // 3
    pairs = width // (2 * HD)
    lanes = 2 * HD
    return pl.pallas_call(
        attend_kernel,
        grid=(1, rows // chunk),
        in_specs=[
            pl.BlockSpec((chunk, lanes), lambda p, i: (i, pair)),
            pl.BlockSpec((rows, lanes), lambda p, i: (0, pairs + pair)),
            pl.BlockSpec((rows, lanes), lambda p, i: (0, 2 * pairs + pair)),
        ],
        out_specs=[
            pl.BlockSpec((chunk, lanes), lambda p, i: (i, 0)),
            pl.BlockSpec((1, 2, chunk), lambda p, i: (0, 0, i)),
        ],
        scratch_shapes=[pltpu.VMEM((lanes, rows), BF)],
        out_shape=[
            jax.ShapeDtypeStruct((rows, lanes), BF),
            jax.ShapeDtypeStruct((1, 2, rows), F32),
        ],
        cost_estimate=pl.CostEstimate(
            flops=48 * rows * rows * lanes, bytes_accessed=8 * rows * lanes, transcendentals=0
        ),
    )(projected, projected, projected)


def attend_back_kernel(
    q_ref, k_ref, v_ref, log_ref, up_ref, dq_ref, dk_ref, dv_ref, turned, key_sum, value_sum
):
    step = pl.program_id(1)

    @pl.when(step == 0)
    def _():
        turned[...] = k_ref[...].T
        key_sum[...] = jnp.zeros_like(key_sum)
        value_sum[...] = jnp.zeros_like(value_sum)

    halves = []
    for head in range(2):
        query = only_head(q_ref[...], head)
        upstream = only_head(up_ref[...], head)
        scores = lax.dot_general(k_ref[...], query, ACROSS, preferred_element_type=F32) * 0.125
        shares = jnp.exp(scores - log_ref[0, head : head + 1, :])
        value_sum[...] += lax.dot_general(
            shares.astype(BF), upstream, PLAIN, preferred_element_type=F32
        )
        slope = lax.dot_general(v_ref[...], upstream, ACROSS, preferred_element_type=F32)
        inner = jnp.sum(shares * slope, axis=0, keepdims=True)
        score_grad = (shares * (slope - inner)).astype(BF)
        key_sum[...] += lax.dot_general(score_grad, query, PLAIN, preferred_element_type=F32)
        keys = turned[head * HD : (head + 1) * HD, :]
        halves.append(lax.dot_general(keys, score_grad, PLAIN, preferred_element_type=F32))
    dq_ref[...] = (jnp.concatenate(halves, axis=0).T * 0.125).astype(BF)

    @pl.when(step == pl.num_programs(1) - 1)
    def _():
        dk_ref[...] = (key_sum[...] * 0.125).astype(BF)
        dv_ref[...] = value_sum[...].astype(BF)


def attention_back(projected, logsum, upstream, pair, chunk):
    rows, columns = projected.shape
    width = columns // 3
    pairs = width // (2 * HD)
    lanes = 2 * HD
    part = pl.BlockSpec((chunk, lanes), lambda p, i: (i, 0))
    whole = pl.BlockSpec((rows, lanes), lambda p, i: (0, 0))
    return pl.pallas_call(
        attend_back_kernel,
        grid=(1, rows // chunk),
        in_specs=[
            pl.BlockSpec((chunk, lanes), lambda p, i: (i, pair)),
            pl.BlockSpec((rows, lanes), lambda p, i: (0, pairs + pair)),
            pl.BlockSpec((rows, lanes), lambda p, i: (0, 2 * pairs + pair)),
            pl.BlockSpec((1, 2, chunk), lambda p, i: (0, 0, i)),
            pl.BlockSpec((chunk, lanes), lambda p, i: (i, pair)),
        ],
        out_specs=[part, whole, whole],
        scratch_shapes=[
            pltpu.VMEM((lanes, rows), BF),
            pltpu.VMEM((rows, lanes), F32),
            pltpu.VMEM((rows, lanes), F32),
        ],
        out_shape=[jax.ShapeDtypeStruct((rows, lanes), BF)] * 3,
        cost_estimate=pl.CostEstimate(
            flops=80 * rows * rows * lanes, bytes_accessed=16 * rows * lanes, transcendentals=0
        ),
    )(projected, projected, projected, logsum, upstream)


def after(value, *others):
    return lax.optimization_barrier((value,) + others)[0]


def on_device(
    image,
    text,
    condition,
    attend_weight,
    output_weight,
    up_weight,
    down_weight,
    adaptive_weight,
    image_cotangent,
    text_cotangent,
):
    width = image.shape[1]
    rows = IMG + TXT
    lay = Layout(width)
    full_width = width * lay.gx
    is_image = (jnp.arange(rows) < IMG)[:, None]

    def per_row(pair):
        return jnp.where(is_image, pair[0][None, :], pair[1][None, :])

    def row_sums(value):
        top = jnp.sum(jnp.where(is_image, value, 0.0), axis=0)
        low = jnp.sum(jnp.where(is_image, 0.0, value), axis=0)
        return jnp.stack([top, low])

    activated = jax.nn.silu(condition.astype(F32)).astype(BF)
    partial_mod = jnp.einsum(
        "sd,qdcx->sqcx", activated, adaptive_weight[0], preferred_element_type=F32
    )
    factors = halve(lay, partial_mod, "gy", lay.me)[0]
    attend_shard = attend_weight[0].reshape(2, lay.rows, 3 * width)
    output_shard = jnp.swapaxes(output_weight[0], 1, 2)
    down_shard = jnp.swapaxes(down_weight[0], 1, 2)
    attend_full = ring_gather(lay, after(attend_shard, factors))
    output_full = ring_gather(lay, after(output_shard, attend_full.arrays[5]))
    up_full = ring_gather(lay, after(up_weight[0], attend_full.arrays[5]))
    down_full = ring_gather(lay, after(down_shard, up_full.arrays[1]))

    shift1, scale1, gate1, shift2, scale2, gate2 = [
        per_row(factors[:, k]) for k in range(6)
    ]

    def totals_of(first, second):
        sums = jnp.stack([jnp.sum(first, axis=1), jnp.sum(second, axis=1)])
        totals = lax.psum(sums, "gx")
        return totals[0][:, None] / full_width, totals[1][:, None] / full_width

    def normalize(value, shift, scale):
        average, square = totals_of(value, value * value)
        inverse = lax.rsqrt(square - average * average + EPSILON)
        unit = (value - average) * inverse
        lowered = (unit * (1.0 + scale) + shift).astype(BF)
        return unit, inverse, spread(lay, lowered)

    def norm_back(grad, unit, inverse, scale):
        scaled = grad * (1.0 + scale)
        mean, inner = totals_of(scaled, scaled * unit)
        return inverse * (scaled - mean - unit * inner)

    stream = jnp.concatenate([image, text], axis=0).astype(F32)
    cotangent = jnp.concatenate([image_cotangent, text_cotangent], axis=0).astype(F32)

    unit1, inverse1, first_full = normalize(stream, shift1, scale1)
    feed_full = spread(lay, (gate2 * cotangent).astype(BF))

    def forward(*rest):
        return forward_product(lay, *rest)

    def backward(*rest):
        return backward_product(lay, *rest)

    def product(*rest):
        return weight_product(lay, *rest)

    pairs = width // (2 * HD)
    projected = forward(first_full, attend_full, width, plain_finish, [BF])[0]
    mixtures, logsums = [], []
    for pair in range(pairs):
        source = after(projected, mixtures[-1]) if mixtures else projected
        mixture, logsum = attention(source, pair, rows)
        mixtures.append(mixture)
        logsums.append(logsum)
    branch = collect(lay, *backward(mixtures, output_full))
    middle = stream + gate1 * branch
    unit2, inverse2, second_full = normalize(middle, shift2, scale2)
    hidden, active = forward(second_full, up_full, 512, gelu_finish, [F32, BF])
    down_grad = ring_scatter(lay, product(feed_full, [active]))

    hidden_grad = forward(feed_full, down_full, 512, slope_finish, [BF], [hidden])[0]
    second_partial = backward([hidden_grad], up_full)
    second_grad = collect(lay, *second_partial)
    up_local = product(second_full, [after(hidden_grad, second_partial[1])])
    up_grad = ring_scatter(lay, up_local)
    middle_grad = cotangent + norm_back(second_grad, unit2, inverse2, scale2)
    branch_full = spread(lay, (gate1 * middle_grad).astype(BF))
    mixed_grad = forward(branch_full, output_full, width, plain_finish, [BF])[0]
    parts = []
    for pair in range(pairs):
        source = after(mixed_grad, parts[-1][0]) if parts else mixed_grad
        parts.append(attention_back(projected, logsums[pair], source, pair, rows))
    projected_grad = [parts[pair][k] for k in range(3) for pair in range(pairs)]
    attend_local = product(first_full, projected_grad)
    attend_grad = ring_scatter(lay, attend_local, 3)
    last_left = after(branch_full[0], attend_local[1])
    output_grad = ring_scatter(lay, product([last_left] + branch_full[1:], mixtures))
    first_partial = backward(projected_grad, attend_full)
    first_grad = collect(lay, *first_partial)
    input_grad = middle_grad + norm_back(first_grad, unit1, inverse1, scale1)

    feed_partial = backward([after(active, first_partial[1])], down_full)
    feed = collect(lay, *feed_partial, late=input_grad)
    result = middle + gate2 * feed

    late = parts[0][0]
    gate2_grad = row_sums(after(cotangent, late) * feed)
    scale2_grad = row_sums(after(second_grad, late) * unit2)
    shift2_grad = row_sums(after(second_grad, late))
    gate1_grad = row_sums(after(middle_grad, late) * branch)
    scale1_grad, shift1_grad = row_sums(first_grad * unit1), row_sums(first_grad)
    modulation_grad = jnp.stack(
        [shift1_grad, scale1_grad, gate1_grad, shift2_grad, scale2_grad, gate2_grad], axis=1
    ).astype(BF)
    all_mod = double(lay, modulation_grad, "gy", lay.me)
    adaptive_grad = jnp.einsum("sd,sqcx->qdcx", activated, all_mod, preferred_element_type=F32)
    condition_partial = jnp.einsum(
        "sqcx,qdcx->sd", all_mod, adaptive_weight[0], preferred_element_type=F32
    )
    share_rows = condition.shape[0] // lay.gx
    condition_share = halve(
        lay, condition_partial.reshape(lay.gx, share_rows, -1), "gx", lay.mx
    )[0]
    own_condition = lax.dynamic_slice_in_dim(condition, lay.mx * share_rows, share_rows, 0)
    _, silu_pullback = jax.vjp(jax.nn.silu, own_condition.astype(F32))
    condition_grad = silu_pullback(condition_share)[0]
    return (
        result[:IMG].astype(BF),
        result[IMG:].astype(BF),
        input_grad[:IMG],
        input_grad[IMG:],
        condition_grad,
        attend_grad[None],
        jnp.swapaxes(output_grad, 1, 2)[None],
        up_grad[None],
        jnp.swapaxes(down_grad, 1, 2)[None],
        adaptive_grad[None],
    )


def solution(mesh):
    placed = (
        P("gy", "gx"),
        P("gy", "gx"),
        P(None, "gy"),
        P(None, None, "gy", None, "gx"),
        P(None, None, "gx", "gy"),
        P(None, None, "gy", "gx"),
        P(None, None, "gx", "gy"),
        P(None, None, "gy", None, "gx"),
        P("gy", "gx"),
        P("gy", "gx"),
    )

    return jax.shard_map(
        on_device,
        mesh=mesh,
        in_specs=placed,
        out_specs=(
            P("gy", "gx"),
            P("gy", "gx"),
            P("gy", "gx"),
            P("gy", "gx"),
            P("gx", "gy"),
            P(None, None, "gy", None, "gx"),
            P(None, None, "gx", "gy"),
            P(None, None, "gy", "gx"),
            P(None, None, "gx", "gy"),
            P(None, None, "gy", None, "gx"),
        ),
        check_vma=False,
    )
```

```python
import functools

import jax
import jax.numpy as jnp
from jax import lax
from jax.experimental import pallas as pl
from jax.experimental.pallas import tpu as pltpu
from jax.sharding import PartitionSpec as P


HD = 64
IMG = 870
TXT = 154
EPSILON = 1e-06


BF = jnp.bfloat16
F32 = jnp.float32


def ring_order(n):
    return [2 * p if p < n // 2 else 2 * (n - 1 - p) + 1 for p in range(n)]


def ring_place(index, n):
    return jnp.where(index % 2 == 0, index // 2, n - 1 - index // 2)


def ring_member(place, n):
    place = place % n
    return jnp.where(place < n // 2, 2 * place, 2 * (n - 1 - place) + 1)


class Layout:
    def __init__(self, width):
        self.n = lax.axis_size("gy")
        self.gx = lax.axis_size("gx")
        self.me = lax.axis_index("gy")
        self.mx = lax.axis_index("gx")
        self.place = ring_place(self.me, self.n)
        self.width = width
        self.rows = width * self.gx // self.n
        order = ring_order(self.n)
        self.cw = [(order[i], order[(i + 1) % self.n]) for i in range(self.n)]
        self.ccw = [(b, a) for a, b in self.cw]

    def offset(self, owner):
        per = self.width // self.rows
        relative = (owner // per) ^ self.mx
        swapped = (relative % 2) * 2 + relative // 2
        return swapped * self.width + (owner % per) * self.rows


class Gathered:
    def __init__(self, arrays, runs):
        self.arrays, self.runs = arrays, runs

    def offsets(self, lay):
        return jnp.stack(
            [lay.offset(owner) + inner for _, _, _, _, owner, inner in self.runs]
        ).astype(jnp.int32)


def first_half(rows):
    return (rows // 2 + 15) // 16 * 16


def ring_gather(lay, shard):
    rows, far = lay.rows, lay.n // 2
    half = first_half(rows)
    arrays, runs = [shard], [(0, (), 0, rows, lay.me, 0)]
    forward = backward = shard
    for k in range(1, far):
        forward = lax.ppermute(forward, "gy", lay.cw)
        backward = lax.ppermute(backward, "gy", lay.ccw)
        runs.append((len(arrays), (), 0, rows, ring_member(lay.place - k + lay.n, lay.n), 0))
        runs.append((len(arrays) + 1, (), 0, rows, ring_member(lay.place + k, lay.n), 0))
        arrays += [forward, backward]
    last = ring_member(lay.place + far, lay.n)
    runs.append((len(arrays), (), 0, half, last, 0))
    runs.append((len(arrays) + 1, (), 0, rows - half, last, half))
    arrays.append(lax.ppermute(forward[:, :half], "gy", lay.cw))
    arrays.append(lax.ppermute(backward[:, half:], "gy", lay.ccw))
    return Gathered(arrays, runs)


def ring_scatter(lay, local, parts=1):
    full, forward, backward = local
    far = lay.n // 2

    def send(forward, backward):
        forward = lax.ppermute(forward, "gy", lay.cw)
        backward = lax.ppermute(backward, "gy", lay.ccw)
        return forward, backward

    forward, backward = send(forward, backward)
    for k in range(far - 1, 0, -1):
        ahead = ring_member(lay.place + k + lay.n, lay.n)
        behind = ring_member(lay.place - k + lay.n, lay.n)
        forward, backward = ring_add(forward, backward, full, ahead, behind)
        forward, backward = send(forward, backward)
    own = lax.dynamic_index_in_dim(full, lay.me, 0, keepdims=False)
    if parts == 1:
        return own.astype(F32) + forward.astype(F32) + backward.astype(F32)
    pieces = zip(*[jnp.split(value, parts, axis=2) for value in (own, forward, backward)])
    return jnp.stack([a.astype(F32) + b.astype(F32) + c.astype(F32) for a, b, c in pieces], axis=2)


def partner(lay, axis, bit):
    size = lay.gx if axis == "gx" else lay.n
    return [(i, i ^ bit) for i in range(size)]


def spread(lay, own):
    across = lax.ppermute(own, "gx", partner(lay, "gx", 2))
    beside = lax.ppermute(own, "gx", partner(lay, "gx", 1))
    beyond = lax.ppermute(across, "gx", partner(lay, "gx", 1))
    return [own, across, beside, beyond]


def collect(lay, kept, sent, late=None):
    w = lay.width
    got = lax.ppermute(sent, "gx", partner(lay, "gx", 1))
    onward = (kept[:, w:].astype(F32) + got[:, w:].astype(F32)).astype(BF)
    across = lax.ppermute(onward, "gx", partner(lay, "gx", 2))
    if late is not None:
        kept, got, across, _ = lax.optimization_barrier((kept, got, across, late))
    return kept[:, :w].astype(F32) + got[:, :w].astype(F32) + across.astype(F32)


def halve(lay, value, axis, index, early=None):
    size, count = value.shape[0], 0
    while size > 1:
        bit = size // 2
        value = value.reshape((2, bit) + value.shape[1:])
        side = (index // bit) % 2
        sent = lax.dynamic_index_in_dim(value, 1 - side, 0, keepdims=False)
        kept = lax.dynamic_index_in_dim(value, side, 0, keepdims=False)
        if count == 1 and early is not None:
            sent = after(sent, early)
        count += 1
        got = lax.ppermute(sent, axis, partner(lay, axis, bit))
        value = kept + got
        size = bit
    return value


def share(lay, value):
    if lay.n > 8:
        return lax.all_gather(value, "gy", axis=0, tiled=False)
    held = [value]
    for k in range(1, lay.n):
        ring = [((i + k) % lay.n, i) for i in range(lay.n)]
        held.append(lax.ppermute(value, "gy", ring))
    held = jnp.stack(held + held, axis=0)
    return lax.dynamic_slice_in_dim(held, (lay.n - lay.me) % lay.n, lay.n, 0)


ACROSS = (((1,), (1,)), ((), ()))
DOWN = (((0,), (0,)), ((), ()))
PLAIN = (((1,), (0,)), ((), ()))
ROOT = 0.7978845608028654
CUBE = 0.044715
LO = IMG // 16 * 16
HI = (IMG + 15) // 16 * 16


def gelu(hidden):
    return 0.5 * hidden * (1.0 + jnp.tanh(ROOT * (hidden + CUBE * (hidden * hidden * hidden))))


def gelu_slope(hidden):
    square = hidden * hidden
    curve = jnp.tanh(ROOT * (hidden + CUBE * (square * hidden)))
    return 0.5 * (1.0 + curve) + 0.5 * hidden * (1.0 - curve * curve) * (
        ROOT * (1.0 + 3.0 * CUBE * square)
    )


def is_image_rows(count):
    return LO + lax.broadcasted_iota(jnp.int32, (HI - LO, count), 0) < IMG


def place_columns(sources, target, sems):
    copies, at = [], 0
    for k, source in enumerate(sources):
        size = source.shape[1]
        copies.append(pltpu.make_async_copy(source, target.at[:, at : at + size], sems.at[k]))
        at += size
    return copies


def store_rows(store, top, low):
    edge = jnp.where(is_image_rows(top.shape[1]), top[LO:HI], low[: HI - LO])
    store(slice(0, LO), top[:LO])
    store(slice(LO, HI), edge)
    store(slice(HI, None), low[HI - LO :])


ANY = pl.BlockSpec(memory_space=pl.ANY)


def forward_kernel(nx, narrays, nextra, runs, tile, finish, offsets, *refs):
    xs, arrays = refs[:nx], refs[nx : nx + narrays]
    extras = refs[nx + narrays : nx + narrays + nextra]
    outs = refs[nx + narrays + nextra : -4]
    xbuf, wbuf, xsem, wsem = refs[-4:]
    step, total = pl.program_id(0), pl.num_programs(0)
    slot = lax.rem(step, 2)

    def fetch(index, slot):
        columns = pl.ds(pl.multiple_of(index * tile, tile), tile)
        for k, (array, lead, row, count) in enumerate(runs):
            pltpu.make_async_copy(
                arrays[array].at[lead + (slice(None), slice(row, row + count), columns)],
                wbuf.at[slot, :, pl.ds(pl.multiple_of(offsets[k], 16), count), :],
                wsem.at[slot],
            ).start()

    @pl.when(step == 0)
    def _():
        for copy in place_columns(xs, xbuf, xsem):
            copy.start()
        fetch(0, 0)

    @pl.when(step + 1 < total)
    def _():
        fetch(step + 1, 1 - slot)

    @pl.when(step == 0)
    def _():
        for copy in place_columns(xs, xbuf, xsem):
            copy.wait()

    pltpu.make_async_copy(wbuf.at[slot], wbuf.at[slot], wsem.at[slot]).wait()
    top = jnp.dot(xbuf[:HI], wbuf[slot, 0], preferred_element_type=F32)
    low = jnp.dot(xbuf[LO:], wbuf[slot, 1], preferred_element_type=F32)
    store_rows(lambda where, value: finish(where, value, extras, outs), top, low)


def plain_finish(where, value, extras, outs):
    outs[0][where, :] = value.astype(outs[0].dtype)


def gelu_finish(where, value, extras, outs):
    outs[0][where, :] = value
    outs[1][where, :] = gelu(value).astype(BF)


def slope_finish(where, value, extras, outs):
    outs[0][where, :] = (gelu_slope(extras[0][where, :]) * value).astype(BF)


def forward_product(lay, xs, weight, tile, finish, out_types, extras=()):
    rows = xs[0].shape[0]
    depth = sum(x.shape[1] for x in xs)
    columns = weight.arrays[0].shape[-1]
    block = pl.BlockSpec((rows, tile), lambda i, _: (0, i))
    return pl.pallas_call(
        functools.partial(
            forward_kernel,
            len(xs),
            len(weight.arrays),
            len(extras),
            [run[:4] for run in weight.runs],
            tile,
            finish,
        ),
        grid_spec=pltpu.PrefetchScalarGridSpec(
            num_scalar_prefetch=1,
            grid=(columns // tile,),
            in_specs=[ANY] * (len(xs) + len(weight.arrays)) + [block] * len(extras),
            out_specs=[block] * len(out_types),
            scratch_shapes=[
                pltpu.VMEM((rows, depth), BF),
                pltpu.VMEM((2, 2, depth, tile), BF),
                pltpu.SemaphoreType.DMA((len(xs),)),
                pltpu.SemaphoreType.DMA((2,)),
            ],
        ),
        out_shape=[jax.ShapeDtypeStruct((rows, columns), dtype) for dtype in out_types],
        cost_estimate=pl.CostEstimate(
            flops=5 * rows * depth * columns,
            bytes_accessed=2 * (rows * depth + 2 * depth * columns + rows * columns),
            transcendentals=0,
        ),
    )(weight.offsets(lay), *xs, *weight.arrays, *extras)


def backward_kernel(nx, narrays, runs, tile, offsets, *refs):
    xs, arrays = refs[:nx], refs[nx : nx + narrays]
    kept, sent = refs[nx + narrays : nx + narrays + 2]
    xbuf, wbuf, xsem, wsem = refs[-4:]
    step, total = pl.program_id(0), pl.num_programs(0)
    half = total // 2
    slot = lax.rem(step, 2)

    def fetch(index, slot):
        first = lax.rem(index + half, total) * tile
        for k, (array, lead, row, count) in enumerate(runs):
            at = offsets[k] - first

            @pl.when(jnp.logical_and(at >= 0, at < tile))
            def _():
                pltpu.make_async_copy(
                    arrays[array].at[lead + (slice(None), slice(row, row + count))],
                    wbuf.at[slot, :, pl.ds(pl.multiple_of(at, 16), count), :],
                    wsem.at[slot],
                ).start()

    @pl.when(step == 0)
    def _():
        for copy in place_columns(xs, xbuf, xsem):
            copy.start()
        fetch(0, 0)

    @pl.when(step + 1 < total)
    def _():
        fetch(step + 1, 1 - slot)

    @pl.when(step == 0)
    def _():
        for copy in place_columns(xs, xbuf, xsem):
            copy.wait()

    pltpu.make_async_copy(wbuf.at[slot], wbuf.at[slot], wsem.at[slot]).wait()
    top = lax.dot_general(xbuf[:HI], wbuf[slot, 0], ACROSS, preferred_element_type=F32)
    low = lax.dot_general(xbuf[LO:], wbuf[slot, 1], ACROSS, preferred_element_type=F32)

    def write(out):
        def store(where, value):
            out[where, :] = value.astype(BF)

        store_rows(store, top, low)

    @pl.when(step < half)
    def _():
        write(sent)

    @pl.when(step >= half)
    def _():
        write(kept)


def backward_product(lay, xs, weight):
    rows = xs[0].shape[0]
    depth = sum(x.shape[1] for x in xs)
    tile = lay.width
    columns = tile * lay.gx
    total = lay.gx
    half = total // 2
    return pl.pallas_call(
        functools.partial(
            backward_kernel,
            len(xs),
            len(weight.arrays),
            [run[:4] for run in weight.runs],
            tile,
        ),
        grid_spec=pltpu.PrefetchScalarGridSpec(
            num_scalar_prefetch=1,
            grid=(total,),
            in_specs=[ANY] * (len(xs) + len(weight.arrays)),
            out_specs=[
                pl.BlockSpec((rows, tile), lambda i, _: (0, jnp.maximum(i - half, 0))),
                pl.BlockSpec((rows, tile), lambda i, _: (0, jnp.minimum(i, half - 1))),
            ],
            scratch_shapes=[
                pltpu.VMEM((rows, depth), BF),
                pltpu.VMEM((2, 2, tile, depth), BF),
                pltpu.SemaphoreType.DMA((len(xs),)),
                pltpu.SemaphoreType.DMA((2,)),
            ],
        ),
        out_shape=[jax.ShapeDtypeStruct((rows, columns // 2), BF)] * 2,
        cost_estimate=pl.CostEstimate(
            flops=5 * rows * depth * columns,
            bytes_accessed=2 * (rows * depth + 2 * depth * columns + rows * columns),
            transcendentals=0,
        ),
    )(weight.offsets(lay), *xs, *weight.arrays)


def weight_kernel(nleft, nright, blocks, *refs):
    lefts, rights = refs[:nleft], refs[nleft : nleft + nright]
    out, ahead, behind, lbuf, rbuf, tbuf, lsem, rsem = refs[nleft + nright :]
    step = pl.program_id(0)

    def left_copies():
        return [
            pltpu.make_async_copy(left, lbuf.at[k], lsem.at[k]) for k, left in enumerate(lefts)
        ]

    @pl.when(step == 0)
    def _():
        first, *others = left_copies()
        for copy in [first] + place_columns(rights, rbuf, rsem) + others:
            copy.start()
        for copy in place_columns(rights, rbuf, rsem):
            copy.wait()
        edge = rbuf[LO:HI]
        image = is_image_rows(edge.shape[1])
        zero = jnp.zeros_like(edge)
        tbuf[: HI - LO] = jnp.where(image, zero, edge)
        tbuf[HI - LO :] = rbuf[HI:]
        rbuf[LO:HI] = jnp.where(image, edge, zero)

    pltpu.make_async_copy(lbuf.at[step], lbuf.at[step], lsem.at[step]).wait()
    top = lax.dot_general(lbuf[step, :HI], rbuf[:HI], DOWN, preferred_element_type=F32)
    low = lax.dot_general(lbuf[step, LO:], tbuf[...], DOWN, preferred_element_type=F32)
    top, low = top.astype(BF), low.astype(BF)
    per, _, count, _ = out.shape
    for k in range(per):
        rows = slice(k * count, (k + 1) * count)
        out[k, 0] = top[rows]
        out[k, 1] = low[rows]

        @pl.when(blocks[step] * per + k == blocks[nleft])
        def _():
            half = ahead.shape[1]
            ahead[0] = top[rows][:half]
            ahead[1] = low[rows][:half]
            behind[0] = top[rows][half:]
            behind[1] = low[rows][half:]


def weight_product(lay, lefts, rights):
    rows, width = lefts[0].shape
    depth = width * len(lefts)
    columns = sum(right.shape[1] for right in rights)
    per = lay.width // lay.rows
    half = first_half(lay.rows)
    last = ring_member(lay.place + lay.n // 2, lay.n)
    blocks = jnp.stack([lay.mx, lay.mx ^ 2, lay.mx ^ 1, lay.mx ^ 3, last]).astype(jnp.int32)
    return pl.pallas_call(
        functools.partial(weight_kernel, len(lefts), len(rights)),
        grid_spec=pltpu.PrefetchScalarGridSpec(
            num_scalar_prefetch=1,
            grid=(len(lefts),),
            in_specs=[ANY] * (len(lefts) + len(rights)),
            out_specs=[
                pl.BlockSpec((per, 2, lay.rows, columns), lambda i, blocks: (blocks[i], 0, 0, 0)),
                pl.BlockSpec((2, half, columns), lambda i, blocks: (0, 0, 0)),
                pl.BlockSpec((2, lay.rows - half, columns), lambda i, blocks: (0, 0, 0)),
            ],
            scratch_shapes=[
                pltpu.VMEM((len(lefts), rows, width), BF),
                pltpu.VMEM((rows, columns), BF),
                pltpu.VMEM((rows - LO, columns), BF),
                pltpu.SemaphoreType.DMA((len(lefts),)),
                pltpu.SemaphoreType.DMA((len(rights),)),
            ],
        ),
        out_shape=[
            jax.ShapeDtypeStruct((lay.n, 2, lay.rows, columns), BF),
            jax.ShapeDtypeStruct((2, half, columns), BF),
            jax.ShapeDtypeStruct((2, lay.rows - half, columns), BF),
        ],
        cost_estimate=pl.CostEstimate(
            flops=5 * rows * depth * columns,
            bytes_accessed=2 * (rows * depth + 2 * depth * columns + rows * columns),
            transcendentals=0,
        ),
    )(blocks, *lefts, *rights)


def add_kernel(owners, forward, backward, ahead, behind, forward_out, backward_out):
    half, other = forward.shape[1], backward.shape[1]
    rows = ahead.shape[2]
    forward_out[0, :half] = forward[0] + ahead[0, 0, :half]
    backward_out[0, rows - other :] = backward[0] + behind[0, 0, rows - other :]
    if half < rows:
        forward_out[0, half:] = ahead[0, 0, half:]
        backward_out[0, : rows - other] = behind[0, 0, : rows - other]


def ring_add(forward, backward, full, ahead, behind):
    _, _, rows, columns = full.shape
    owners = jnp.stack([ahead, behind]).astype(jnp.int32)

    def moving(value):
        return pl.BlockSpec((1, value.shape[1], columns), lambda s, _: (s, 0, 0))

    out = pl.BlockSpec((1, rows, columns), lambda s, _: (s, 0, 0))
    return pl.pallas_call(
        add_kernel,
        grid_spec=pltpu.PrefetchScalarGridSpec(
            num_scalar_prefetch=1,
            grid=(2,),
            in_specs=[
                moving(forward),
                moving(backward),
                pl.BlockSpec((1, 1, rows, columns), lambda s, owners: (owners[0], s, 0, 0)),
                pl.BlockSpec((1, 1, rows, columns), lambda s, owners: (owners[1], s, 0, 0)),
            ],
            out_specs=[out, out],
        ),
        out_shape=[jax.ShapeDtypeStruct((2, rows, columns), BF)] * 2,
        cost_estimate=pl.CostEstimate(
            flops=10000 * rows * columns, bytes_accessed=24 * rows * columns, transcendentals=0
        ),
    )(owners, forward, backward, full, full)


def only_head(block, head):
    lane = lax.broadcasted_iota(jnp.int32, block.shape, 1)
    return jnp.where(lane // HD == head, block, jnp.zeros_like(block))


def attend_kernel(q_ref, k_ref, v_ref, mix_ref, log_ref, turned):
    @pl.when(pl.program_id(1) == 0)
    def _():
        turned[...] = v_ref[...].T

    halves = []
    for head in range(2):
        query = only_head(q_ref[...], head)
        scores = lax.dot_general(k_ref[...], query, ACROSS, preferred_element_type=F32) * 0.125
        highest = jnp.max(scores, axis=0, keepdims=True)
        powers = jnp.exp(scores - highest)
        total = jnp.sum(powers, axis=0, keepdims=True)
        shares = (powers * (1.0 / total)).astype(BF)
        values = turned[head * HD : (head + 1) * HD, :]
        halves.append(lax.dot_general(values, shares, PLAIN, preferred_element_type=F32))
        log_ref[0, head : head + 1, :] = highest + jnp.log(total)
    mix_ref[...] = jnp.concatenate(halves, axis=0).T.astype(BF)


def attention(projected, pair, chunk):
    rows, columns = projected.shape
    width = columns // 3
    pairs = width // (2 * HD)
    lanes = 2 * HD
    return pl.pallas_call(
        attend_kernel,
        grid=(1, rows // chunk),
        in_specs=[
            pl.BlockSpec((chunk, lanes), lambda p, i: (i, pair)),
            pl.BlockSpec((rows, lanes), lambda p, i: (0, pairs + pair)),
            pl.BlockSpec((rows, lanes), lambda p, i: (0, 2 * pairs + pair)),
        ],
        out_specs=[
            pl.BlockSpec((chunk, lanes), lambda p, i: (i, 0)),
            pl.BlockSpec((1, 2, chunk), lambda p, i: (0, 0, i)),
        ],
        scratch_shapes=[pltpu.VMEM((lanes, rows), BF)],
        out_shape=[
            jax.ShapeDtypeStruct((rows, lanes), BF),
            jax.ShapeDtypeStruct((1, 2, rows), F32),
        ],
        cost_estimate=pl.CostEstimate(
            flops=48 * rows * rows * lanes, bytes_accessed=8 * rows * lanes, transcendentals=0
        ),
    )(projected, projected, projected)


def attend_back_kernel(
    q_ref, k_ref, v_ref, log_ref, up_ref, dq_ref, dk_ref, dv_ref, turned, key_sum, value_sum
):
    step = pl.program_id(1)

    @pl.when(step == 0)
    def _():
        turned[...] = k_ref[...].T
        key_sum[...] = jnp.zeros_like(key_sum)
        value_sum[...] = jnp.zeros_like(value_sum)

    halves = []
    for head in range(2):
        query = only_head(q_ref[...], head)
        upstream = only_head(up_ref[...], head)
        scores = lax.dot_general(k_ref[...], query, ACROSS, preferred_element_type=F32) * 0.125
        shares = jnp.exp(scores - log_ref[0, head : head + 1, :])
        value_sum[...] += lax.dot_general(
            shares.astype(BF), upstream, PLAIN, preferred_element_type=F32
        )
        slope = lax.dot_general(v_ref[...], upstream, ACROSS, preferred_element_type=F32)
        inner = jnp.sum(shares * slope, axis=0, keepdims=True)
        score_grad = (shares * (slope - inner)).astype(BF)
        key_sum[...] += lax.dot_general(score_grad, query, PLAIN, preferred_element_type=F32)
        keys = turned[head * HD : (head + 1) * HD, :]
        halves.append(lax.dot_general(keys, score_grad, PLAIN, preferred_element_type=F32))
    dq_ref[...] = (jnp.concatenate(halves, axis=0).T * 0.125).astype(BF)

    @pl.when(step == pl.num_programs(1) - 1)
    def _():
        dk_ref[...] = (key_sum[...] * 0.125).astype(BF)
        dv_ref[...] = value_sum[...].astype(BF)


def attention_back(projected, logsum, upstream, pair, chunk):
    rows, columns = projected.shape
    width = columns // 3
    pairs = width // (2 * HD)
    lanes = 2 * HD
    part = pl.BlockSpec((chunk, lanes), lambda p, i: (i, 0))
    whole = pl.BlockSpec((rows, lanes), lambda p, i: (0, 0))
    return pl.pallas_call(
        attend_back_kernel,
        grid=(1, rows // chunk),
        in_specs=[
            pl.BlockSpec((chunk, lanes), lambda p, i: (i, pair)),
            pl.BlockSpec((rows, lanes), lambda p, i: (0, pairs + pair)),
            pl.BlockSpec((rows, lanes), lambda p, i: (0, 2 * pairs + pair)),
            pl.BlockSpec((1, 2, chunk), lambda p, i: (0, 0, i)),
            pl.BlockSpec((chunk, lanes), lambda p, i: (i, pair)),
        ],
        out_specs=[part, whole, whole],
        scratch_shapes=[
            pltpu.VMEM((lanes, rows), BF),
            pltpu.VMEM((rows, lanes), F32),
            pltpu.VMEM((rows, lanes), F32),
        ],
        out_shape=[jax.ShapeDtypeStruct((rows, lanes), BF)] * 3,
        cost_estimate=pl.CostEstimate(
            flops=80 * rows * rows * lanes, bytes_accessed=16 * rows * lanes, transcendentals=0
        ),
    )(projected, projected, projected, logsum, upstream)


def after(value, *others):
    return lax.optimization_barrier((value,) + others)[0]


def on_device(
    image,
    text,
    condition,
    attend_weight,
    output_weight,
    up_weight,
    down_weight,
    adaptive_weight,
    image_cotangent,
    text_cotangent,
):
    width = image.shape[1]
    rows = IMG + TXT
    lay = Layout(width)
    full_width = width * lay.gx
    is_image = (jnp.arange(rows) < IMG)[:, None]

    def per_row(pair):
        return jnp.where(is_image, pair[0][None, :], pair[1][None, :])

    def row_sums(value):
        top = jnp.sum(jnp.where(is_image, value, 0.0), axis=0)
        low = jnp.sum(jnp.where(is_image, 0.0, value), axis=0)
        return jnp.stack([top, low])

    activated = jax.nn.silu(condition.astype(F32)).astype(BF)
    partial_mod = jnp.einsum(
        "sd,qdcx->sqcx", activated, adaptive_weight[0], preferred_element_type=F32
    )
    attend_shard = attend_weight[0].reshape(2, lay.rows, 3 * width)
    factors = halve(lay, partial_mod, "gy", lay.me, attend_shard)[0]
    output_shard = jnp.swapaxes(output_weight[0], 1, 2)
    down_shard = jnp.swapaxes(down_weight[0], 1, 2)
    attend_full = ring_gather(lay, attend_shard)
    output_full = ring_gather(lay, after(output_shard, attend_full.arrays[5]))
    up_full = ring_gather(lay, after(up_weight[0], attend_full.arrays[5]))
    down_full = ring_gather(lay, after(down_shard, up_full.arrays[1]))

    shift1, scale1, gate1, shift2, scale2, gate2 = [
        per_row(factors[:, k]) for k in range(6)
    ]

    def totals_of(first, second):
        sums = jnp.stack([jnp.sum(first, axis=1), jnp.sum(second, axis=1)])
        totals = lax.psum(sums, "gx")
        return totals[0][:, None] / full_width, totals[1][:, None] / full_width

    def normalize(value, shift, scale):
        average, square = totals_of(value, value * value)
        inverse = lax.rsqrt(square - average * average + EPSILON)
        unit = (value - average) * inverse
        lowered = (unit * (1.0 + scale) + shift).astype(BF)
        return unit, inverse, spread(lay, lowered)

    def norm_back(grad, unit, inverse, scale):
        scaled = grad * (1.0 + scale)
        mean, inner = totals_of(scaled, scaled * unit)
        return inverse * (scaled - mean - unit * inner)

    stream = jnp.concatenate([image, text], axis=0).astype(F32)
    cotangent = jnp.concatenate([image_cotangent, text_cotangent], axis=0).astype(F32)

    unit1, inverse1, first_full = normalize(stream, shift1, scale1)
    feed_full = spread(lay, (gate2 * cotangent).astype(BF))

    def forward(*rest):
        return forward_product(lay, *rest)

    def backward(*rest):
        return backward_product(lay, *rest)

    def product(*rest):
        return weight_product(lay, *rest)

    pairs = width // (2 * HD)
    projected = forward(first_full, attend_full, width, plain_finish, [BF])[0]
    mixtures, logsums = [], []
    for pair in range(pairs):
        source = after(projected, mixtures[-1]) if mixtures else projected
        mixture, logsum = attention(source, pair, rows)
        mixtures.append(mixture)
        logsums.append(logsum)
    branch = collect(lay, *backward(mixtures, output_full))
    middle = stream + gate1 * branch
    unit2, inverse2, second_full = normalize(middle, shift2, scale2)
    hidden, active = forward(second_full, up_full, 512, gelu_finish, [F32, BF])
    down_grad = ring_scatter(lay, product(feed_full, [active]))

    hidden_grad = forward(feed_full, down_full, 512, slope_finish, [BF], [hidden])[0]
    second_partial = backward([hidden_grad], up_full)
    second_grad = collect(lay, *second_partial)
    up_local = product(second_full, [after(hidden_grad, second_partial[1])])
    up_grad = ring_scatter(lay, up_local)
    middle_grad = cotangent + norm_back(second_grad, unit2, inverse2, scale2)
    branch_full = spread(lay, (gate1 * middle_grad).astype(BF))
    mixed_grad = forward(branch_full, output_full, width, plain_finish, [BF])[0]
    parts = []
    for pair in range(pairs):
        source = after(mixed_grad, parts[-1][0]) if parts else mixed_grad
        parts.append(attention_back(projected, logsums[pair], source, pair, rows))
    projected_grad = [parts[pair][k] for k in range(3) for pair in range(pairs)]
    attend_local = product(first_full, projected_grad)
    attend_grad = ring_scatter(lay, attend_local, 3)
    last_left = after(branch_full[0], attend_local[1])
    output_grad = ring_scatter(lay, product([last_left] + branch_full[1:], mixtures))
    first_partial = backward(projected_grad, attend_full)
    first_grad = collect(lay, *first_partial)
    input_grad = middle_grad + norm_back(first_grad, unit1, inverse1, scale1)

    feed_partial = backward([after(active, first_partial[1])], down_full)
    feed = collect(lay, *feed_partial, late=input_grad)
    result = middle + gate2 * feed

    late = parts[0][0]
    gate2_grad = row_sums(after(cotangent, late) * feed)
    scale2_grad = row_sums(after(second_grad, late) * unit2)
    shift2_grad = row_sums(after(second_grad, late))
    gate1_grad = row_sums(after(middle_grad, late) * branch)
    scale1_grad, shift1_grad = row_sums(first_grad * unit1), row_sums(first_grad)
    modulation_grad = jnp.stack(
        [shift1_grad, scale1_grad, gate1_grad, shift2_grad, scale2_grad, gate2_grad], axis=1
    ).astype(BF)
    all_mod = share(lay, modulation_grad)
    adaptive_grad = jnp.einsum("sd,sqcx->qdcx", activated, all_mod, preferred_element_type=F32)
    condition_partial = jnp.einsum(
        "sqcx,qdcx->sd", all_mod, adaptive_weight[0], preferred_element_type=F32
    )
    share_rows = condition.shape[0] // lay.gx
    condition_share = halve(lay, condition_partial.reshape(lay.gx, share_rows, -1), "gx", lay.mx)[0]
    own_condition = lax.dynamic_slice_in_dim(condition, lay.mx * share_rows, share_rows, 0)
    _, silu_pullback = jax.vjp(jax.nn.silu, own_condition.astype(F32))
    condition_grad = silu_pullback(condition_share)[0]
    return (
        result[:IMG].astype(BF),
        result[IMG:].astype(BF),
        input_grad[:IMG],
        input_grad[IMG:],
        condition_grad,
        attend_grad[None],
        jnp.swapaxes(output_grad, 1, 2)[None],
        up_grad[None],
        jnp.swapaxes(down_grad, 1, 2)[None],
        adaptive_grad[None],
    )


def solution(mesh):
    placed = (
        P("gy", "gx"),
        P("gy", "gx"),
        P(None, "gy"),
        P(None, None, "gy", None, "gx"),
        P(None, None, "gx", "gy"),
        P(None, None, "gy", "gx"),
        P(None, None, "gx", "gy"),
        P(None, None, "gy", None, "gx"),
        P("gy", "gx"),
        P("gy", "gx"),
    )

    return jax.shard_map(
        on_device,
        mesh=mesh,
        in_specs=placed,
        out_specs=(
            P("gy", "gx"),
            P("gy", "gx"),
            P("gy", "gx"),
            P("gy", "gx"),
            P("gx", "gy"),
            P(None, None, "gy", None, "gx"),
            P(None, None, "gx", "gy"),
            P(None, None, "gy", "gx"),
            P(None, None, "gx", "gy"),
            P(None, None, "gy", None, "gx"),
        ),
        check_vma=False,
    )
```
